32 devices in a mesh: seq: 2 (over y), row: 4 (over x, core), col: 4 (over z).
Axes of the slice: x: 2, y: 2, z: 4, core: 2. Of those that a mesh axis runs over, the one named last changes fastest.
Arguments:
- tokens: bfloat16 [4096, 5376], P(('seq', 'row'), 'col'), may hold values from -6 to 6
- w_query: bfloat16 [5376, 4096], P(('seq', 'row'), 'col'), may hold values from -0.078125 to 0.078125
- key_weight: bfloat16 [5376, 2048], P(('seq', 'row'), 'col'), may hold values from -0.078125 to 0.078125
- value_weight: bfloat16 [5376, 2048], P(('seq', 'row'), 'col'), may hold values from -0.078125 to 0.078125
- w_output: bfloat16 [4096, 5376], P(('seq', 'row'), 'col'), may hold values from -0.09375 to 0.09375
- query_gain: float32 [128], replicated, may hold values from 0.5 to 8
- key_gain: float32 [128], replicated, may hold values from 0.5 to 8
Outputs:
- attended: bfloat16 [4096, 5376], P(('seq', 'row'), 'col')
The draws below stay inside these ranges and needn't reach their ends.
All inputs are finite; a program needn't handle non-finite values.
Results may differ from the reference program's by a relative error of at most 0.0085.
The reference program's roundings to bfloat16 on the way count: a program that leaves them out, or rounds other values in their place, can miss the bound.
Values may be sent and summed in bfloat16 or wider, within the bound.
A program may use at most 128 MiB of HBM per device.

```python
import jax
import jax.numpy as jnp
from jax import lax

MODEL_WIDTH = 5376
HQ = 32
KEY_VALUE_HEADS = 16
HEAD_SIZE = 128
WINDOW_KEYS = 1024
TOK_DEV = 512
TOKENS = 4096


def draw_query_gain(key, part):
    local = jax.random.fold_in(key, 11)
    return jax.random.uniform(local, (HEAD_SIZE,), jnp.float32, 0.5, 1.5)


def draw_key_gain(key, part):
    local = jax.random.fold_in(key, 12)
    return jax.random.uniform(local, (HEAD_SIZE,), jnp.float32, 0.5, 1.5)


def block_levels(own_key, extent, pieces, smallest, high):
    level = 1.0
    for axis_at, shards_of in pieces:
        draws = jax.random.uniform(jax.random.fold_in(jax.random.fold_in(own_key, 6), axis_at), (shards_of,), jnp.float32, smallest / len(pieces), high / len(pieces))
        level = level * jnp.repeat(jnp.exp(draws), extent[axis_at] // shards_of).reshape((-1,) + (1,) * (len(extent) - 1 - axis_at))
    return level


def centred(stream_key, shape, width, most, shards=(), kind=jnp.bfloat16):
    drawn = width * jax.random.normal(stream_key, shape, jnp.float32)
    if shards:
        drawn = drawn * block_levels(stream_key, shape, shards, -0.22, 0.18)
    return jnp.clip(drawn, -most, most).astype(kind)


def setup_inputs(seed: int = 0) -> dict:
    keys = jax.random.split(jax.random.key(seed), 8)
    return {
        "tokens": centred(keys[0], (TOKENS, MODEL_WIDTH), 1.0, 6.0, ((0, 8), (1, 4))),
        "w_query": centred(keys[1], (MODEL_WIDTH, HQ * HEAD_SIZE), MODEL_WIDTH ** -0.5, 0.078125, ((0, 8), (1, 4))),
        "key_weight": centred(keys[2], (MODEL_WIDTH, KEY_VALUE_HEADS * HEAD_SIZE), MODEL_WIDTH ** -0.5, 0.078125, ((0, 8), (1, 4))),
        "value_weight": centred(keys[3], (MODEL_WIDTH, KEY_VALUE_HEADS * HEAD_SIZE), MODEL_WIDTH ** -0.5, 0.078125, ((0, 8), (1, 4))),
        "w_output": centred(keys[4], (HQ * HEAD_SIZE, MODEL_WIDTH), (HQ * HEAD_SIZE) ** -0.5, 0.09375, ((0, 8), (1, 4))),
        "query_gain": draw_query_gain(jax.random.fold_in(keys[7], 71), 0),
        "key_gain": draw_key_gain(jax.random.fold_in(keys[7], 71), 0),
    }


query_scale = 168.0 ** (-0.5)

def head_norm(block, gain):
    mean_square = lax.optimization_barrier(jnp.mean(block * block, axis=-1, keepdims=True))
    return block * lax.rsqrt(mean_square + 1e-06) * gain

def rotate(block, positions):
    half = block.shape[-1] // 2
    freqs = 10000.0 ** (-(jnp.arange(half, dtype=jnp.float32) * 2.0 / block.shape[-1]))
    angles = positions.astype(jnp.float32)[:, None] * freqs[None, :]
    cosine = jnp.cos(angles)[:, None, :]
    sine = jnp.sin(angles)[:, None, :]
    first = block[..., :half]
    second = block[..., half:]
    return jnp.concatenate([first * cosine - second * sine, second * cosine + first * sine], axis=-1)

def attend(queries, key_states, value_states, qpos, kpos):
    rows = queries.shape[0]
    kv_heads = key_states.shape[1]
    grouped = queries.astype(jnp.float32).reshape(rows, kv_heads, 2, HEAD_SIZE)
    scores = jnp.einsum('bhgd,khd->hgbk', grouped, key_states.astype(jnp.float32)) * query_scale
    gap = qpos[:, None] - kpos[None, :]
    valid = (kpos[None, :] >= 0) & (gap >= 0) & (gap < WINDOW_KEYS)
    scores = jnp.where(valid[None, None], scores, -1e+30)
    top = lax.optimization_barrier(jnp.max(scores, axis=-1, keepdims=True))
    weights = jnp.exp(scores - top)
    weights = (weights / lax.optimization_barrier(jnp.sum(weights, axis=-1, keepdims=True))).astype(jnp.bfloat16)
    mixed = jnp.einsum('hgbk,khd->bhgd', weights.astype(jnp.float32), value_states.astype(jnp.float32))
    return mixed.astype(jnp.bfloat16).reshape(rows, kv_heads * 2 * HEAD_SIZE)

def reference(tokens, w_query, key_weight, value_weight, w_output, query_gain, key_gain):
    total_length = tokens.shape[0]
    positions = jnp.arange(total_length, dtype=jnp.int32)
    proj_q = jnp.dot(tokens, w_query, preferred_element_type=jnp.float32).reshape(total_length, HQ, HEAD_SIZE)
    projected_key = jnp.dot(tokens, key_weight, preferred_element_type=jnp.float32).reshape(total_length, KEY_VALUE_HEADS, HEAD_SIZE)
    value_states = jnp.dot(tokens, value_weight, preferred_element_type=jnp.float32).astype(jnp.bfloat16).reshape(total_length, KEY_VALUE_HEADS, HEAD_SIZE)
    queries = rotate(head_norm(proj_q, query_gain), positions).astype(jnp.bfloat16)
    key_states = rotate(head_norm(projected_key, key_gain), positions).astype(jnp.bfloat16)
    block = TOK_DEV
    count = total_length // block
    key_padded_rows = jnp.concatenate([jnp.zeros((WINDOW_KEYS, KEY_VALUE_HEADS, HEAD_SIZE), jnp.bfloat16), key_states], axis=0)
    value_padded_rows = jnp.concatenate([jnp.zeros((WINDOW_KEYS, KEY_VALUE_HEADS, HEAD_SIZE), jnp.bfloat16), value_states], axis=0)

    def one_block(index):
        start = (index * block).astype(jnp.int32)
        query_rows = lax.dynamic_slice_in_dim(queries, start, block, 0)
        key_rows = lax.dynamic_slice_in_dim(key_padded_rows, start, block + WINDOW_KEYS, 0)
        value_rows = lax.dynamic_slice_in_dim(value_padded_rows, start, block + WINDOW_KEYS, 0)
        qpos = start + jnp.arange(block, dtype=jnp.int32)
        kpos = start - WINDOW_KEYS + jnp.arange(block + WINDOW_KEYS, dtype=jnp.int32)
        return attend(query_rows, key_rows, value_rows, qpos, kpos)
    mixed = lax.map(one_block, jnp.arange(count, dtype=jnp.int32)).reshape(total_length, HQ * HEAD_SIZE)
    return jnp.dot(mixed, w_output, preferred_element_type=jnp.float32).astype(jnp.bfloat16)
```

```python
import jax
import jax.numpy as jnp
from jax import lax
from jax.experimental import pallas as pl
from jax.experimental.pallas import tpu as pltpu
from jax.sharding import PartitionSpec as P

HEAD_SIZE = 128
WINDOW_KEYS = 1024


query_scale = 168.0 ** (-0.5)


def shifted(block, axis, distance):
    devices = range(lax.axis_size(axis))
    route = [(i - distance, i) for i in devices if i - distance in devices]
    return lax.ppermute(block, axis, route)


def head_norm(block, gain):
    mean_square = jnp.mean(block * block, axis=-1, keepdims=True)
    return block * lax.rsqrt(mean_square + 1e-06) * gain


def rotate(block, positions):
    half = block.shape[-1] // 2
    freqs = 10000.0 ** (-(jnp.arange(half, dtype=jnp.float32) * 2.0 / block.shape[-1]))
    angles = positions.astype(jnp.float32)[:, None] * freqs[None, :]
    cosine = jnp.cos(angles)[:, None, :]
    sine = jnp.sin(angles)[:, None, :]
    first = block[..., :half]
    second = block[..., half:]
    return jnp.concatenate(
        [first * cosine - second * sine, second * cosine + first * sine], axis=-1
    )


def attend(queries, key_states, value_states, qpos, kpos):
    rows = queries.shape[0]
    kv_heads = key_states.shape[1]
    grouped = queries.reshape(rows, kv_heads, 2, HEAD_SIZE)
    scores = (
        jnp.einsum("bhgd,khd->hgbk", grouped, key_states, preferred_element_type=jnp.float32)
        * query_scale
    )
    gap = qpos[:, None] - kpos[None, :]
    valid = (kpos[None, :] >= 0) & (gap >= 0) & (gap < WINDOW_KEYS)
    scores = jnp.where(valid[None, None], scores, -1e30)
    top = jnp.max(scores, axis=-1, keepdims=True)
    weights = jnp.exp(scores - top)
    weights = (weights / jnp.sum(weights, axis=-1, keepdims=True)).astype(jnp.bfloat16)
    mixed = jnp.einsum("hgbk,khd->bhgd", weights, value_states, preferred_element_type=jnp.float32)
    return mixed.astype(jnp.bfloat16).reshape(rows, kv_heads * 2 * HEAD_SIZE)


def shards(tokens, w_query, key_weight, value_weight, w_output, query_gain, key_gain):
    rows = tokens.shape[0]
    whole = lax.all_gather(tokens, "col", axis=1, tiled=True)
    columns = whole
    proj_q = jnp.dot(
        columns,
        lax.all_gather(w_query, ("seq", "row"), axis=0, tiled=True),
        preferred_element_type=jnp.float32,
    )
    projected_key = jnp.dot(
        columns,
        lax.all_gather(key_weight, ("seq", "row"), axis=0, tiled=True),
        preferred_element_type=jnp.float32,
    )
    proj_v = jnp.dot(
        columns,
        lax.all_gather(value_weight, ("seq", "row"), axis=0, tiled=True),
        preferred_element_type=jnp.float32,
    )
    base = lax.axis_index(("seq", "row")) * rows
    positions = base + jnp.arange(rows, dtype=jnp.int32)
    q_heads = proj_q.shape[1] // HEAD_SIZE
    kv_heads = projected_key.shape[1] // HEAD_SIZE
    queries = rotate(
        head_norm(proj_q.reshape(rows, q_heads, HEAD_SIZE), query_gain), positions
    ).astype(jnp.bfloat16)
    key_states = rotate(
        head_norm(projected_key.reshape(rows, kv_heads, HEAD_SIZE), key_gain), positions
    ).astype(jnp.bfloat16)
    key_flat = key_states.reshape(rows, kv_heads * HEAD_SIZE)
    value_flat = proj_v.astype(jnp.bfloat16)
    prior_one = shifted((key_flat, value_flat), ("seq", "row"), 1)
    prior_two = shifted((key_flat, value_flat), ("seq", "row"), 2)
    key_rows = jnp.concatenate([prior_two[0], prior_one[0], key_flat], axis=0).reshape(
        3 * rows, kv_heads, HEAD_SIZE
    )
    value_rows = jnp.concatenate([prior_two[1], prior_one[1], value_flat], axis=0).reshape(
        3 * rows, kv_heads, HEAD_SIZE
    )
    kpos = base - 2 * rows + jnp.arange(3 * rows, dtype=jnp.int32)
    mixed = attend(queries, key_rows, value_rows, positions, kpos)
    all_heads = lax.all_gather(mixed, "col", axis=1, tiled=True)
    columns = all_heads
    attended = jnp.dot(
        columns,
        lax.all_gather(w_output, ("seq", "row"), axis=0, tiled=True),
        preferred_element_type=jnp.float32,
    )
    return attended.astype(jnp.bfloat16)


MESH = pl.DeviceIdType.MESH
MIB = 1 << 20
SENDS = 14
LOG2_E = 1.4426950408889634


class Place:
    def __init__(self):
        self.y = lax.axis_index("seq")
        row = lax.axis_index("row")
        self.x, self.c = row // 2, row % 2
        self.z = lax.axis_index("col")
        self.to_x = {"seq": self.y, "row": (1 - self.x) * 2 + self.c, "col": self.z}
        self.to_y = {"seq": 1 - self.y, "row": row, "col": self.z}
        self.to_c = {"seq": self.y, "row": self.x * 2 + 1 - self.c, "col": self.z}
        self.up = {"seq": self.y, "row": row, "col": self.z + 1}
        self.down = {"seq": self.y, "row": row, "col": self.z - 1}
        self.to_d = {"seq": 1 - self.y, "row": (1 - self.x) * 2 + self.c, "col": self.z}
        self.chip = self.y * 2 + self.x
        after = (self.chip + 1) % 4
        self.after = {"seq": after // 2, "row": (after % 2) * 2 + self.c, "col": self.z}
        self.chip_x = self.y * 2 + 1 - self.x
        self.chip_y = (1 - self.y) * 2 + self.x
        self.chip_d = (1 - self.y) * 2 + 1 - self.x


def barrier(at):
    sem = pltpu.get_barrier_semaphore()
    for device in (at.to_x, at.to_y, at.to_c, at.to_d):
        pl.semaphore_signal(sem, inc=1, device_id=device, device_id_type=MESH)

    @pl.when(at.z < 3)
    def _():
        pl.semaphore_signal(sem, inc=1, device_id=at.up, device_id_type=MESH)

    @pl.when(at.z > 0)
    def _():
        pl.semaphore_signal(sem, inc=1, device_id=at.down, device_id_type=MESH)

    peers = 4 + (at.z < 3).astype(jnp.int32) + (at.z > 0).astype(jnp.int32)
    pl.semaphore_wait(sem, peers)


class Line:
    def __init__(self, at, part, send, recv):
        self.at, self.part, self.send, self.recv = at, part, send, recv

    def copy(self, block, part, way):
        piece = self.part(block, part)
        return pltpu.make_async_remote_copy(
            src_ref=piece, dst_ref=piece,
            send_sem=self.send.at[way, block, part], recv_sem=self.recv.at[block, part],
            device_id=self.at.up if way == 0 else self.at.down, device_id_type=MESH)

    def start(self, part):
        at = self.at

        @pl.when(at.z < 3)
        def _():
            self.copy(at.z, part, 0).start()

        @pl.when(at.z > 0)
        def _():
            self.copy(at.z, part, 1).start()

    def rising(self, s, part):
        at = self.at

        @pl.when(at.z - s >= 0)
        def _():
            self.copy(at.z - s, part, 0).wait_recv()

            @pl.when(at.z < 3)
            def _():
                self.copy(at.z - s, part, 0).start()

    def falling(self, s, part):
        at = self.at

        @pl.when(at.z + s <= 3)
        def _():
            self.copy(at.z + s, part, 1).wait_recv()

            @pl.when(at.z > 0)
            def _():
                self.copy(at.z + s, part, 1).start()

    def step(self, s, part):
        self.rising(s, part)
        self.falling(s, part)

    def finish(self, parts):
        at = self.at
        for s in range(4):
            for part in range(parts):
                @pl.when((at.z - s >= 0) & (at.z < 3))
                def _():
                    self.copy(at.z - s, part, 0).wait_send()

                @pl.when((at.z + s <= 3) & (at.z > 0))
                def _():
                    self.copy(at.z + s, part, 1).wait_send()


class Plane:
    def __init__(self, at, part, send, recv):
        self.at, self.part, self.send, self.recv = at, part, send, recv
        self.plan = [
            (at.chip, 0, at.to_x), (at.chip, 1, at.to_y),
            (at.chip, 0, at.to_c), (at.chip, 1, at.to_c),
            (at.chip, 1, at.to_x), (at.chip, 0, at.to_y),
            (at.chip_x, 0, at.to_y), (at.chip_x, 0, at.to_c),
            (at.chip_y, 1, at.to_x), (at.chip_y, 1, at.to_c),
            (at.chip_x, 1, at.to_c), (at.chip_y, 0, at.to_c),
            (at.chip_d, 0, at.to_c), (at.chip_d, 1, at.to_c),
        ]

    def copy(self, chip, core, half, device, slot):
        piece = self.part(chip * 2 + core, half)
        return pltpu.make_async_remote_copy(
            src_ref=piece, dst_ref=piece,
            send_sem=self.send.at[slot], recv_sem=self.recv.at[chip * 2 + core, half],
            device_id=device, device_id_type=MESH)

    def push(self, slot):
        chip, half, device = self.plan[slot]
        return self.copy(chip, self.at.c, half, device, slot)

    def send_slots(self, low, high):
        for slot in range(low, high):
            self.push(slot).start()

    def need(self, chip, core, half):
        self.copy(chip, core, half, self.at.to_c, 0).wait_recv()

    def begin(self):
        self.send_slots(0, 4)

    def rest(self):
        self.send_slots(4, 6)

    def start(self):
        self.begin()
        self.rest()

    def first(self):
        at = self.at
        self.need(at.chip_x, at.c, 0)
        self.send_slots(6, 8)
        self.need(at.chip_y, at.c, 1)
        self.send_slots(8, 10)

    def second(self):
        at = self.at
        self.need(at.chip_x, at.c, 1)
        self.send_slots(10, 11)
        self.need(at.chip_y, at.c, 0)
        self.send_slots(11, 12)

    def third(self):
        at = self.at
        for half in range(2):
            self.need(at.chip_d, at.c, half)
            self.send_slots(12 + half, 13 + half)
        for half in range(2):
            for chip in (at.chip, at.chip_x, at.chip_y, at.chip_d):
                self.need(chip, 1 - at.c, half)

    def finish(self):
        for slot in range(SENDS):
            self.push(slot).wait_send()


class Halo:
    def __init__(self, at, kv, rows, sems):
        self.at, self.kv, self.rows, self.sems = at, kv, rows, sems

    def piece(self, block, h):
        cols = pl.ds(pl.multiple_of(h * 256, 256), 256)
        return self.kv.at[pl.ds(block * self.rows, self.rows), cols]

    def on(self, h):
        return pltpu.make_async_remote_copy(
            src_ref=self.piece(2, h), dst_ref=self.piece(0, h),
            send_sem=self.sems.at[0, h], recv_sem=self.sems.at[1, h],
            device_id=self.at.after, device_id_type=MESH)

    def across(self, block, h):
        return pltpu.make_async_remote_copy(
            src_ref=self.piece(block, h), dst_ref=self.piece(1, h),
            send_sem=self.sems.at[2, h], recv_sem=self.sems.at[3, h],
            device_id=self.at.to_c, device_id_type=MESH)

    def start(self, h):
        @pl.when(self.at.chip < 3)
        def _():
            self.on(h).start()

        @pl.when(self.at.c == 0)
        def _():
            self.across(2, h).start()

    def need(self, h):
        at = self.at

        @pl.when(at.chip > 0)
        def _():
            self.on(h).wait_recv()

            @pl.when(at.c == 1)
            def _():
                self.across(0, h).start()

        @pl.when((at.chip > 0) | (at.c == 1))
        def _():
            self.across(0, h).wait_recv()

    def finish(self, h):
        at = self.at

        @pl.when(at.chip < 3)
        def _():
            self.on(h).wait_send()

        @pl.when((at.chip > 0) | (at.c == 0))
        def _():
            self.across(0, h).wait_send()


def kernel(x, wq, wk, wv, wo, gain_q, gain_k, freqs, out,
           x_all, turned, w_kv, w_q, total, part_q, o_all, mixed, kv, q, total_o, mask, result,
           cosine, sine,
           zs, zr, ks, kr, qs, qr, ms, mr, os, orr, hs, local):
    at = Place()
    depth, rows = x.shape
    nq, nk = wq.shape[1], wk.shape[1]
    features = wo.shape[0]
    heads = nk // 128
    shard = depth // 2
    device = at.chip * 2 + at.c
    outer = (at.z == 0) | (at.z == 3)
    inner = jnp.logical_not(outer)
    mine = pl.ds(pl.multiple_of(device * shard, 16), shard)
    load_x = pltpu.make_async_copy(x, x_all.at[at.z], local.at[0])
    load_kv = [
        pltpu.make_async_copy(wk, w_kv.at[mine, pl.ds(0, nk)], local.at[1]),
        pltpu.make_async_copy(wv, w_kv.at[mine, pl.ds(nk, nk)], local.at[2]),
    ]
    load_q = [
        pltpu.make_async_copy(wq.at[:, pl.ds(h * 256, 256)], w_q.at[h, mine], local.at[3 + h])
        for h in range(heads)
    ]
    load_o = pltpu.make_async_copy(wo, o_all.at[device], local.at[7])
    for load in [load_x] + load_kv + load_q:
        load.start()
    barrier(at)
    half = rows // 2
    wide = features // 2

    def kv_part(index, h):
        start = pl.multiple_of(index * shard + h * (shard // 2), 16)
        return w_kv.at[pl.ds(start, shard // 2)]

    def q_part(head):
        def part(index, h):
            start = pl.multiple_of(index * shard + h * (shard // 2), 16)
            return w_q.at[head, pl.ds(start, shard // 2)]
        return part

    def o_part(tile):
        def part(index, h):
            return o_all.at[index, pl.ds(tile * wide + h * (wide // 2), wide // 2)]
        return part

    line = Line(at, lambda b, p: x_all.at[b, pl.ds(p * shard, shard)], zs, zr)
    line_m = Line(at, lambda b, p: mixed.at[b, :, pl.ds(p * 256, 256)], ms, mr)
    plane_k = Plane(at, kv_part, ks, kr)
    plane_q = [Plane(at, q_part(h), qs.at[h], qr.at[h]) for h in range(heads)]
    plane_o = [Plane(at, o_part(t), os.at[t], orr.at[t]) for t in range(2)]
    halo = Halo(at, kv, rows, hs)

    def apart(distance):
        return lambda j: (j - at.z == distance) | (at.z - j == distance)

    def project(j, p):
        @pl.loop(0, 2 * nk // 256)
        def _(tile):
            cols = pl.ds(pl.multiple_of(tile * 256, 256), 256)
            start = pl.multiple_of((j * 2 + p) * shard, 16)
            total[:, cols] += jnp.dot(
                turned[j * 2 + p], w_kv[pl.ds(start, shard), cols],
                preferred_element_type=jnp.float32)

    def each(which, parts, *steps):
        @pl.loop(0, 4)
        def _(j):
            @pl.when(which(j))
            def _():
                for p in parts:
                    for step in steps:
                        step(j, p)

    def turn(j, p):
        turned[j * 2 + p] = x_all[j, p * shard:(p + 1) * shard, :].T

    load_x.wait()
    line.start(0)
    for load in load_kv:
        load.wait()
    plane_k.start()
    line.start(1)
    load_o.start()
    turn(at.z, 0)
    turn(at.z, 1)
    total[...] = jnp.zeros_like(total)
    total_o[...] = jnp.zeros_like(total_o)

    @pl.when(at.chip == 0)
    def _():
        kv[pl.ds(0, rows), :] = jnp.zeros((rows, 2 * nk), jnp.bfloat16)

        @pl.when(at.c == 0)
        def _():
            kv[pl.ds(rows, rows), :] = jnp.zeros((rows, 2 * nk), jnp.bfloat16)

    for load in load_q:
        load.wait()
    load_o.wait()

    plane_k.first()
    plane_q[0].start()
    plane_q[1].start()
    line.step(1, 0)

    positions = device * rows + lax.broadcasted_iota(jnp.int32, (rows, 128), 0)
    angles = positions.astype(jnp.float32) * freqs[...]
    lower = lax.broadcasted_iota(jnp.int32, (rows, 128), 1) < 64
    cosine[...] = jnp.cos(angles)
    turned_sine = jnp.sin(angles)
    sine[...] = jnp.where(lower, -turned_sine, turned_sine)

    span = half + 2 * rows
    for tile in range(2):
        query = lax.broadcasted_iota(jnp.int32, (half, span), 0)
        key = lax.broadcasted_iota(jnp.int32, (half, span), 1)
        low = 2 * rows - device * rows - tile * half
        valid = (key > query) & (key <= query + WINDOW_KEYS) & (key >= low)
        mask[tile] = jnp.where(valid, 0.0, -1e30)

    each(apart(1), (0,), turn)
    plane_k.second()
    line.step(1, 1)
    each(apart(1), (1,), turn)
    line.step(2, 0)
    plane_k.third()
    each(apart(0), (0, 1), project)
    each(apart(1), (0, 1), project)
    plane_q[0].first()
    plane_q[0].second()
    each(apart(2), (0,), turn, project)
    line.step(2, 1)
    plane_q[1].first()

    @pl.when(outer)
    def _():
        plane_q[2].start()
        plane_q[3].start()

    each(apart(2), (1,), turn, project)
    plane_q[0].third()
    plane_q[1].second()

    @pl.when(outer)
    def _():
        plane_q[1].third()
        line.step(3, 0)

    each(apart(3), (0,), turn, project)

    @pl.when(outer)
    def _():
        plane_q[2].first()
        plane_q[2].second()
        plane_q[3].first()
        plane_o[0].begin()
        plane_q[3].second()
        plane_q[2].third()
        line.step(3, 1)

    each(apart(3), (1,), turn, project)

    def head(block, gain):
        mean_square = jnp.mean(block * block, axis=-1, keepdims=True)
        normed = block * lax.rsqrt(mean_square + 1e-06) * gain
        spun = normed * cosine[...] + pltpu.roll(normed, 64, 1) * sine[...]
        return spun.astype(jnp.bfloat16)

    own = pl.ds(2 * rows, rows)

    @pl.loop(0, heads)
    def _(h):
        keys = total[:, pl.ds(pl.multiple_of(h * 128, 128), 128)]
        kv[own, pl.ds(pl.multiple_of(h * 256, 256), 128)] = head(keys, gain_k[...])
        values = total[:, pl.ds(pl.multiple_of(nk + h * 128, 128), 128)]
        kv[own, pl.ds(pl.multiple_of(h * 256 + 128, 128), 128)] = values.astype(jnp.bfloat16)
        halo.start(h)

    @pl.when(inner)
    def _():
        plane_q[2].start()
        plane_q[1].third()

    @pl.when(outer)
    def _():
        plane_o[0].rest()
        plane_q[3].third()

    def project_q(h):
        part_q[...] = jnp.zeros_like(part_q)

        @pl.loop(0, 8)
        def _(i):
            start = pl.multiple_of(i * shard, 16)
            part_q[...] += jnp.dot(
                turned[i], w_q[h, pl.ds(start, shard), :], preferred_element_type=jnp.float32)

        for g in range(2):
            q[:, g * 128:(g + 1) * 128] = head(part_q[:, g * 128:(g + 1) * 128], gain_q[...])

    def attend_head(h):
        @pl.loop(0, 2)
        def _(tile):
            first = pl.multiple_of(tile * half, half)
            keys = kv[pl.ds(first, span), h * 256:h * 256 + 128]
            values = kv[pl.ds(first, span), h * 256 + 128:h * 256 + 256]
            for g in range(2):
                cols = slice(g * 128, (g + 1) * 128)
                scores = lax.dot_general(
                    q[pl.ds(first, half), cols], keys, (((1,), (1,)), ((), ())),
                    preferred_element_type=jnp.float32)
                scores = scores + mask[tile]
                top = jnp.max(scores, axis=-1, keepdims=True)
                weights = jnp.exp2((scores - top) * (query_scale * LOG2_E))
                inverse = 1.0 / jnp.sum(weights, axis=-1, keepdims=True)
                weights = (weights * inverse).astype(jnp.bfloat16)
                cols = slice((2 * h + g) * 128, (2 * h + g + 1) * 128)
                mixed[at.z, pl.ds(first, half), cols] = jnp.dot(
                    weights, values, preferred_element_type=jnp.float32).astype(jnp.bfloat16)

    def relay_inner(h):
        @pl.when(at.z == 1)
        def _():
            line_m.falling(1, h)

        @pl.when(at.z == 2)
        def _():
            line_m.rising(1, h)

    def relay_outer(s, h):
        @pl.when(at.z == (1 if s == 1 else 2))
        def _():
            line_m.rising(s, h)

        @pl.when(at.z == (2 if s == 1 else 1))
        def _():
            line_m.falling(s, h)

    for h in range(heads):
        project_q(h)
        if h == 0:
            @pl.when(outer)
            def _():
                plane_o[0].first()
                plane_o[1].begin()
                plane_o[1].rest()
        halo.need(h)
        attend_head(h)
        line_m.start(h)

        @pl.when(inner)
        def _():
            if h > 0:
                relay_inner(h - 1)
            if h == 1:
                plane_q[2].first()
                plane_q[3].start()
                plane_q[2].second()
                plane_q[2].third()
            if h == 2:
                plane_q[3].first()
                plane_o[0].start()
                plane_q[3].second()
                plane_q[3].third()
            if h == 3:
                plane_o[0].first()
                plane_o[1].start()

        if h == 2:
            @pl.when(outer)
            def _():
                plane_o[0].second()
                plane_o[0].third()

    def output(tile, p):
        some = pl.ds(tile * wide, wide)

        def step(j, _):
            total_o[some, :] += lax.dot_general(
                o_all[j * 2 + p, some, :], mixed[j, :, p * (nq // 2):(p + 1) * (nq // 2)],
                (((1,), (1,)), ((), ())), preferred_element_type=jnp.float32)
        return step

    last = jnp.where(at.z < 2, 3, 0)

    @pl.when(inner)
    def _():
        relay_inner(heads - 1)
        relay_outer(1, 0)
        relay_outer(1, 1)
        relay_outer(2, 0)
        plane_o[0].second()
        plane_o[0].third()
        relay_outer(1, 2)
        relay_outer(2, 1)
        relay_outer(1, 3)
        relay_outer(2, 2)

    @pl.when(outer)
    def _():
        for s in (1, 2):
            for h in range(heads):
                line_m.step(s, h)

    plane_o[1].first()
    for p in range(2):
        each(lambda j: j != last, (0,), output(0, p))
    plane_o[1].second()
    plane_o[1].third()

    @pl.when(inner)
    def _():
        relay_outer(2, 3)

    for p in range(2):
        each(lambda j: j != last, (0,), output(1, p))

    line_m.step(3, 0)
    line_m.step(3, 1)
    each(lambda j: j == last, (0,), output(0, 0), output(1, 0))
    line_m.step(3, 2)
    line_m.step(3, 3)
    stores = []
    for tile in range(2):
        some = pl.ds(tile * wide, wide)
        rest = lax.dot_general(
            o_all[last * 2 + 1, some, :], mixed[last, :, nq // 2:],
            (((1,), (1,)), ((), ())), preferred_element_type=jnp.float32)
        result[some, :] = (total_o[some, :] + rest).astype(jnp.bfloat16)
        stores.append(pltpu.make_async_copy(result.at[some], out.at[some], local.at[8 + tile]))
        stores[-1].start()
    line.finish(2)
    line_m.finish(heads)
    for plane in [plane_k] + plane_q + plane_o:
        plane.finish()
    for h in range(heads):
        halo.finish(h)
    for store in stores:
        store.wait()


def fused(tokens, w_query, key_weight, value_weight, w_output, query_gain, key_gain):
    rows, depth = tokens.shape
    nq, nk = w_query.shape[1], key_weight.shape[1]
    features = w_output.shape[1]
    freqs = 10000.0 ** (-(jnp.arange(64, dtype=jnp.float32) * 2.0 / HEAD_SIZE))
    freqs = jnp.concatenate([freqs, freqs]).reshape(1, HEAD_SIZE)
    hbm = pl.BlockSpec(memory_space=pl.ANY)
    vmem = pl.BlockSpec(memory_space=pltpu.VMEM)
    bf16, dma = jnp.bfloat16, pltpu.SemaphoreType.DMA
    return pl.pallas_call(
        kernel,
        out_shape=jax.ShapeDtypeStruct((features, rows), bf16),
        in_specs=[hbm] * 5 + [vmem] * 3,
        out_specs=hbm,
        scratch_shapes=[
            pltpu.VMEM((4, depth, rows), bf16),
            pltpu.VMEM((8, rows, depth // 2), bf16),
            pltpu.VMEM((4 * depth, 2 * nk), bf16),
            pltpu.VMEM((nq // 256, 4 * depth, 256), bf16),
            pltpu.VMEM((rows, 2 * nk), jnp.float32),
            pltpu.VMEM((rows, 256), jnp.float32),
            pltpu.VMEM((8, features, nq // 2), bf16),
            pltpu.VMEM((4, rows, nq), bf16),
            pltpu.VMEM((3 * rows, 2 * nk), bf16),
            pltpu.VMEM((rows, 256), bf16),
            pltpu.VMEM((features, rows), jnp.float32),
            pltpu.VMEM((2, rows // 2, rows // 2 + WINDOW_KEYS), jnp.float32),
            pltpu.VMEM((features, rows), bf16),
            pltpu.VMEM((rows, HEAD_SIZE), jnp.float32),
            pltpu.VMEM((rows, HEAD_SIZE), jnp.float32),
            dma((2, 4, 2)), dma((4, 2)),
            dma((SENDS,)), dma((8, 2)), dma((4, SENDS)), dma((4, 8, 2)),
            dma((2, 4, 4)), dma((4, 4)), dma((2, SENDS)), dma((2, 8, 2)),
            dma((4, 4)), dma((10,)),
        ],
        compiler_params=pltpu.CompilerParams(
            collective_id=0, has_side_effects=True, vmem_limit_bytes=62 * MIB),
    )(tokens.T, w_query, key_weight, value_weight, w_output.T,
      query_gain.reshape(1, HEAD_SIZE), key_gain.reshape(1, HEAD_SIZE), freqs).T


def solution(mesh):
    small = dict(mesh.shape) == {"seq": 2, "row": 4, "col": 4}
    split = P(("seq", "row"), "col")
    return jax.shard_map(
        fused if small else shards,
        mesh=mesh,
        in_specs=(split, split, split, split, split, P(), P()),
        out_specs=split,
        check_vma=False,
    )
```

```python
import jax
import jax.numpy as jnp
from jax import lax
from jax.experimental import pallas as pl
from jax.experimental.pallas import tpu as pltpu
from jax.sharding import PartitionSpec as P

HEAD_SIZE = 128
WINDOW_KEYS = 1024


query_scale = 168.0 ** (-0.5)


def shifted(block, axis, distance):
    devices = range(lax.axis_size(axis))
    route = [(i - distance, i) for i in devices if i - distance in devices]
    return lax.ppermute(block, axis, route)


def head_norm(block, gain):
    mean_square = jnp.mean(block * block, axis=-1, keepdims=True)
    return block * lax.rsqrt(mean_square + 1e-06) * gain


def rotate(block, positions):
    half = block.shape[-1] // 2
    freqs = 10000.0 ** (-(jnp.arange(half, dtype=jnp.float32) * 2.0 / block.shape[-1]))
    angles = positions.astype(jnp.float32)[:, None] * freqs[None, :]
    cosine = jnp.cos(angles)[:, None, :]
    sine = jnp.sin(angles)[:, None, :]
    first = block[..., :half]
    second = block[..., half:]
    return jnp.concatenate(
        [first * cosine - second * sine, second * cosine + first * sine], axis=-1
    )


def attend(queries, key_states, value_states, qpos, kpos):
    rows = queries.shape[0]
    kv_heads = key_states.shape[1]
    grouped = queries.reshape(rows, kv_heads, 2, HEAD_SIZE)
    scores = (
        jnp.einsum("bhgd,khd->hgbk", grouped, key_states, preferred_element_type=jnp.float32)
        * query_scale
    )
    gap = qpos[:, None] - kpos[None, :]
    valid = (kpos[None, :] >= 0) & (gap >= 0) & (gap < WINDOW_KEYS)
    scores = jnp.where(valid[None, None], scores, -1e30)
    top = jnp.max(scores, axis=-1, keepdims=True)
    weights = jnp.exp(scores - top)
    weights = (weights / jnp.sum(weights, axis=-1, keepdims=True)).astype(jnp.bfloat16)
    mixed = jnp.einsum("hgbk,khd->bhgd", weights, value_states, preferred_element_type=jnp.float32)
    return mixed.astype(jnp.bfloat16).reshape(rows, kv_heads * 2 * HEAD_SIZE)


def shards(tokens, w_query, key_weight, value_weight, w_output, query_gain, key_gain):
    rows = tokens.shape[0]
    whole = lax.all_gather(tokens, "col", axis=1, tiled=True)
    columns = whole
    proj_q = jnp.dot(
        columns,
        lax.all_gather(w_query, ("seq", "row"), axis=0, tiled=True),
        preferred_element_type=jnp.float32,
    )
    projected_key = jnp.dot(
        columns,
        lax.all_gather(key_weight, ("seq", "row"), axis=0, tiled=True),
        preferred_element_type=jnp.float32,
    )
    proj_v = jnp.dot(
        columns,
        lax.all_gather(value_weight, ("seq", "row"), axis=0, tiled=True),
        preferred_element_type=jnp.float32,
    )
    base = lax.axis_index(("seq", "row")) * rows
    positions = base + jnp.arange(rows, dtype=jnp.int32)
    q_heads = proj_q.shape[1] // HEAD_SIZE
    kv_heads = projected_key.shape[1] // HEAD_SIZE
    queries = rotate(
        head_norm(proj_q.reshape(rows, q_heads, HEAD_SIZE), query_gain), positions
    ).astype(jnp.bfloat16)
    key_states = rotate(
        head_norm(projected_key.reshape(rows, kv_heads, HEAD_SIZE), key_gain), positions
    ).astype(jnp.bfloat16)
    key_flat = key_states.reshape(rows, kv_heads * HEAD_SIZE)
    value_flat = proj_v.astype(jnp.bfloat16)
    prior_one = shifted((key_flat, value_flat), ("seq", "row"), 1)
    prior_two = shifted((key_flat, value_flat), ("seq", "row"), 2)
    key_rows = jnp.concatenate([prior_two[0], prior_one[0], key_flat], axis=0).reshape(
        3 * rows, kv_heads, HEAD_SIZE
    )
    value_rows = jnp.concatenate([prior_two[1], prior_one[1], value_flat], axis=0).reshape(
        3 * rows, kv_heads, HEAD_SIZE
    )
    kpos = base - 2 * rows + jnp.arange(3 * rows, dtype=jnp.int32)
    mixed = attend(queries, key_rows, value_rows, positions, kpos)
    all_heads = lax.all_gather(mixed, "col", axis=1, tiled=True)
    columns = all_heads
    attended = jnp.dot(
        columns,
        lax.all_gather(w_output, ("seq", "row"), axis=0, tiled=True),
        preferred_element_type=jnp.float32,
    )
    return attended.astype(jnp.bfloat16)


MESH = pl.DeviceIdType.MESH
MIB = 1 << 20
LOG2_E = 1.4426950408889634


class Place:
    def __init__(self):
        self.y = lax.axis_index("seq")
        row = lax.axis_index("row")
        self.x, self.c = row // 2, row % 2
        self.z = lax.axis_index("col")
        self.to_x = {"seq": self.y, "row": (1 - self.x) * 2 + self.c, "col": self.z}
        self.to_y = {"seq": 1 - self.y, "row": row, "col": self.z}
        self.to_c = {"seq": self.y, "row": self.x * 2 + 1 - self.c, "col": self.z}
        self.up = {"seq": self.y, "row": row, "col": self.z + 1}
        self.down = {"seq": self.y, "row": row, "col": self.z - 1}
        self.to_d = {"seq": 1 - self.y, "row": (1 - self.x) * 2 + self.c, "col": self.z}
        self.chip = self.y * 2 + self.x
        after = (self.chip + 1) % 4
        self.after = {"seq": after // 2, "row": (after % 2) * 2 + self.c, "col": self.z}
        self.chip_x = self.y * 2 + 1 - self.x
        self.chip_y = (1 - self.y) * 2 + self.x
        self.chip_d = (1 - self.y) * 2 + 1 - self.x


def barrier(at):
    sem = pltpu.get_barrier_semaphore()
    for device in (at.to_x, at.to_y, at.to_c, at.to_d):
        pl.semaphore_signal(sem, inc=1, device_id=device, device_id_type=MESH)

    @pl.when(at.z < 3)
    def _():
        pl.semaphore_signal(sem, inc=1, device_id=at.up, device_id_type=MESH)

    @pl.when(at.z > 0)
    def _():
        pl.semaphore_signal(sem, inc=1, device_id=at.down, device_id_type=MESH)

    peers = 4 + (at.z < 3).astype(jnp.int32) + (at.z > 0).astype(jnp.int32)
    pl.semaphore_wait(sem, peers)


class Line:
    def __init__(self, at, whole, part, send, recv):
        self.at, self.whole, self.part, self.send, self.recv = at, whole, part, send, recv

    def copy(self, block, part, way):
        piece = self.part(block, part)
        return pltpu.make_async_remote_copy(
            src_ref=piece, dst_ref=piece,
            send_sem=self.send.at[way], recv_sem=self.recv.at[block, part],
            device_id=self.at.up if way == 0 else self.at.down, device_id_type=MESH)

    def start(self, part):
        at = self.at

        @pl.when(at.z < 3)
        def _():
            self.copy(at.z, part, 0).start()

        @pl.when(at.z > 0)
        def _():
            self.copy(at.z, part, 1).start()

    def rising(self, s, part):
        at = self.at

        @pl.when(at.z - s >= 0)
        def _():
            self.copy(at.z - s, part, 0).wait_recv()

            @pl.when(at.z < 3)
            def _():
                self.copy(at.z - s, part, 0).start()

    def falling(self, s, part):
        at = self.at

        @pl.when(at.z + s <= 3)
        def _():
            self.copy(at.z + s, part, 1).wait_recv()

            @pl.when(at.z > 0)
            def _():
                self.copy(at.z + s, part, 1).start()

    def step(self, s, part):
        self.rising(s, part)
        self.falling(s, part)

    def sent(self, way, blocks):
        piece = self.whole.at[pl.ds(0, blocks)]
        pltpu.make_async_remote_copy(
            src_ref=piece, dst_ref=piece,
            send_sem=self.send.at[way], recv_sem=self.recv.at[0, 0],
            device_id=self.at.up if way == 0 else self.at.down, device_id_type=MESH).wait_send()

    def finish(self):
        for z in range(4):
            @pl.when(self.at.z == z)
            def _():
                if z < 3:
                    self.sent(0, z + 1)
                if z > 0:
                    self.sent(1, 4 - z)


class Plane:
    def __init__(self, at, shards, cut, send, recv):
        self.at, self.shards, self.cut, self.send, self.recv = at, shards, cut, send, recv

    def copy(self, piece, device, slot):
        return pltpu.make_async_remote_copy(
            src_ref=piece, dst_ref=piece, send_sem=self.send.at[0],
            recv_sem=self.recv.at[slot], device_id=device, device_id_type=MESH)

    def half(self, chip, h):
        return self.cut(chip * 2 + self.at.c, h)

    def push(self, chip, h, device, slot):
        self.copy(self.half(chip, h), device, slot).start()

    def share(self, chip):
        self.copy(self.shards(chip * 2 + self.at.c, 1), self.at.to_c, 4).start()

    def need(self, piece, slot):
        self.copy(piece, self.at.to_c, slot).wait_recv()

    def begin(self):
        at = self.at
        self.push(at.chip, 0, at.to_x, 0)
        self.push(at.chip, 1, at.to_y, 1)
        self.share(at.chip)

    def rest(self):
        at = self.at
        self.push(at.chip, 1, at.to_x, 2)
        self.push(at.chip, 0, at.to_y, 2)

    def start(self):
        self.begin()
        self.rest()

    def first(self):
        at = self.at
        self.need(self.half(at.chip_x, 0), 0)
        self.push(at.chip_x, 0, at.to_y, 3)
        self.need(self.half(at.chip_y, 1), 1)
        self.push(at.chip_y, 1, at.to_x, 3)

    def second(self):
        at = self.at
        self.need(self.shards(0, 1), 2)
        self.share(at.chip_x)
        self.share(at.chip_y)

    def third(self):
        at = self.at
        self.need(self.shards(0, 1), 3)
        self.share(at.chip_d)
        self.need(self.shards(0, 4), 4)

    def finish(self):
        self.copy(self.shards(0, 7), self.at.to_c, 0).wait_send()


class Halo:
    def __init__(self, at, kv, rows, send, recv):
        self.at, self.kv, self.rows, self.send, self.recv = at, kv, rows, send, recv

    def piece(self, block, h):
        cols = pl.ds(pl.multiple_of(h * 256, 256), 256)
        return self.kv.at[pl.ds(block * self.rows, self.rows), cols]

    def on(self, h):
        return pltpu.make_async_remote_copy(
            src_ref=self.piece(2, h), dst_ref=self.piece(0, h),
            send_sem=self.send.at[0], recv_sem=self.recv.at[0, h],
            device_id=self.at.after, device_id_type=MESH)

    def across(self, block, h):
        return pltpu.make_async_remote_copy(
            src_ref=self.piece(block, h), dst_ref=self.piece(1, h),
            send_sem=self.send.at[1], recv_sem=self.recv.at[1, h],
            device_id=self.at.to_c, device_id_type=MESH)

    def start(self, h):
        @pl.when(self.at.chip < 3)
        def _():
            self.on(h).start()

        @pl.when(self.at.c == 0)
        def _():
            self.across(2, h).start()

    def need(self, h):
        at = self.at

        @pl.when(at.chip > 0)
        def _():
            self.on(h).wait_recv()

            @pl.when(at.c == 1)
            def _():
                self.across(0, h).start()

        @pl.when((at.chip > 0) | (at.c == 1))
        def _():
            self.across(0, h).wait_recv()

    def sent(self, way):
        block = self.kv.at[pl.ds(0, self.rows)]
        pltpu.make_async_remote_copy(
            src_ref=block, dst_ref=block, send_sem=self.send.at[way],
            recv_sem=self.recv.at[0, 0], device_id=self.at.to_c, device_id_type=MESH).wait_send()

    def finish(self):
        at = self.at

        @pl.when(at.chip < 3)
        def _():
            self.sent(0)

        @pl.when((at.chip > 0) | (at.c == 0))
        def _():
            self.sent(1)


def kernel(x, wq, wk, wv, wo, query_gain, key_gain, freqs, out,
           x_all, turned, w_kv, w_q, total, part_q, o_all, mixed, kv, q, total_o, mask,
           cosine, sine, gain_q, gain_k, steps,
           zs, zr, ks, kr, qs, qr, ms, mr, os, orr, hs, hr, local):
    at = Place()
    depth, rows = x.shape
    nq, nk = wq.shape[1], wk.shape[1]
    features = wo.shape[0]
    heads = nk // 128
    shard = depth // 2
    device = at.chip * 2 + at.c
    outer = (at.z == 0) | (at.z == 3)
    inner = jnp.logical_not(outer)
    mine = pl.ds(pl.multiple_of(device * shard, 16), shard)
    load_x = pltpu.make_async_copy(x, x_all.at[at.z], local.at[0])
    load_kv = [
        pltpu.make_async_copy(wk, w_kv.at[mine, pl.ds(0, nk)], local.at[1]),
        pltpu.make_async_copy(wv, w_kv.at[mine, pl.ds(nk, nk)], local.at[2]),
    ]
    load_q = [
        pltpu.make_async_copy(wq.at[:, pl.ds(h * 256, 256)], w_q.at[h, mine], local.at[3])
        for h in range(heads)
    ]
    loads_q = pltpu.make_async_copy(w_q.at[:, mine], w_q.at[:, mine], local.at[3])
    load_o = pltpu.make_async_copy(wo, o_all.at[device], local.at[4])
    load_small = [
        pltpu.make_async_copy(query_gain, gain_q, local.at[5]),
        pltpu.make_async_copy(key_gain, gain_k, local.at[6]),
        pltpu.make_async_copy(freqs, steps, local.at[7]),
    ]
    for load in [load_x] + load_kv + load_q + load_small:
        load.start()
    barrier(at)
    half = rows // 2
    wide = features // 2

    def kv_cut(index, h):
        start = pl.multiple_of(index * shard + h * (shard // 2), 16)
        return w_kv.at[pl.ds(start, shard // 2)]

    def kv_shards(index, n):
        return w_kv.at[pl.ds(pl.multiple_of(index * shard, 16), n * shard)]

    def q_cut(head):
        def piece(index, h):
            start = pl.multiple_of(index * shard + h * (shard // 2), 16)
            return w_q.at[head, pl.ds(start, shard // 2)]
        return piece

    def q_shards(head):
        def piece(index, n):
            return w_q.at[head, pl.ds(pl.multiple_of(index * shard, 16), n * shard)]
        return piece

    def o_cut(tile):
        def piece(index, h):
            return o_all.at[index, pl.ds(tile * wide + h * (wide // 2), wide // 2)]
        return piece

    def o_shards(tile):
        def piece(index, n):
            return o_all.at[pl.ds(index, n), pl.ds(tile * wide, wide)]
        return piece

    line = Line(at, x_all, lambda b, p: x_all.at[b, pl.ds(p * shard, shard)], zs, zr)
    line_m = Line(at, mixed, lambda b, p: mixed.at[b, :, pl.ds(p * 256, 256)], ms, mr)
    plane_k = Plane(at, kv_shards, kv_cut, ks, kr)
    plane_q = [Plane(at, q_shards(h), q_cut(h), qs.at[h], qr.at[h]) for h in range(heads)]
    plane_o = [Plane(at, o_shards(t), o_cut(t), os.at[t], orr.at[t]) for t in range(2)]
    halo = Halo(at, kv, rows, hs, hr)

    def apart(distance):
        return lambda j: (j - at.z == distance) | (at.z - j == distance)

    def project(j, p):
        @pl.loop(0, 2 * nk // 256)
        def _(tile):
            cols = pl.ds(pl.multiple_of(tile * 256, 256), 256)
            start = pl.multiple_of((j * 2 + p) * shard, 16)
            total[:, cols] += jnp.dot(
                turned[j * 2 + p], w_kv[pl.ds(start, shard), cols],
                preferred_element_type=jnp.float32)

    def each(which, parts, *steps):
        @pl.loop(0, 4)
        def _(j):
            @pl.when(which(j))
            def _():
                for p in parts:
                    for step in steps:
                        step(j, p)

    def turn(j, p):
        turned[j * 2 + p] = x_all[j, p * shard:(p + 1) * shard, :].T

    load_x.wait()
    line.start(0)
    for load in load_kv:
        load.wait()
    plane_k.start()
    line.start(1)
    load_o.start()
    turn(at.z, 0)
    turn(at.z, 1)
    total[...] = jnp.zeros_like(total)
    total_o[...] = jnp.zeros_like(total_o)

    @pl.when(at.chip == 0)
    def _():
        kv[pl.ds(0, rows), :] = jnp.zeros((rows, 2 * nk), jnp.bfloat16)

        @pl.when(at.c == 0)
        def _():
            kv[pl.ds(rows, rows), :] = jnp.zeros((rows, 2 * nk), jnp.bfloat16)

    loads_q.wait()
    load_o.wait()
    for load in load_small:
        load.wait()

    plane_k.first()
    plane_q[0].start()
    plane_q[1].start()
    line.step(1, 0)

    positions = device * rows + lax.broadcasted_iota(jnp.int32, (rows, 128), 0)
    angles = positions.astype(jnp.float32) * jnp.concatenate([steps[...], steps[...]], axis=1)
    lower = lax.broadcasted_iota(jnp.int32, (rows, 128), 1) < 64
    cosine[...] = jnp.cos(angles)
    turned_sine = jnp.sin(angles)
    sine[...] = jnp.where(lower, -turned_sine, turned_sine)

    span = half + 2 * rows
    for tile in range(2):
        query = lax.broadcasted_iota(jnp.int32, (half, span), 0)
        key = lax.broadcasted_iota(jnp.int32, (half, span), 1)
        low = 2 * rows - device * rows - tile * half
        valid = (key > query) & (key <= query + WINDOW_KEYS) & (key >= low)
        mask[tile] = jnp.where(valid, 0.0, -1e30)

    each(apart(1), (0,), turn)
    plane_k.second()
    line.step(1, 1)
    each(apart(1), (1,), turn)
    line.step(2, 0)
    plane_k.third()
    each(apart(0), (0, 1), project)
    each(apart(1), (0, 1), project)
    plane_q[0].first()
    plane_q[0].second()
    each(apart(2), (0,), turn, project)
    line.step(2, 1)
    plane_q[1].first()

    @pl.when(outer)
    def _():
        plane_q[2].start()
        plane_q[3].start()

    each(apart(2), (1,), turn, project)
    plane_q[0].third()
    plane_q[1].second()

    @pl.when(outer)
    def _():
        plane_q[1].third()
        line.step(3, 0)

    each(apart(3), (0,), turn, project)

    @pl.when(outer)
    def _():
        plane_q[2].first()
        plane_q[2].second()
        plane_q[3].first()
        plane_o[0].begin()
        plane_q[3].second()
        plane_q[2].third()
        line.step(3, 1)

    each(apart(3), (1,), turn, project)

    def head(block, gain):
        mean_square = jnp.mean(block * block, axis=-1, keepdims=True)
        normed = block * lax.rsqrt(mean_square + 1e-06) * gain
        spun = normed * cosine[...] + pltpu.roll(normed, 64, 1) * sine[...]
        return spun.astype(jnp.bfloat16)

    own = pl.ds(2 * rows, rows)

    @pl.loop(0, heads)
    def _(h):
        keys = total[:, pl.ds(pl.multiple_of(h * 128, 128), 128)]
        kv[own, pl.ds(pl.multiple_of(h * 256, 256), 128)] = head(keys, gain_k[...])
        values = total[:, pl.ds(pl.multiple_of(nk + h * 128, 128), 128)]
        kv[own, pl.ds(pl.multiple_of(h * 256 + 128, 128), 128)] = values.astype(jnp.bfloat16)
        halo.start(h)

    @pl.when(inner)
    def _():
        plane_q[2].start()
        plane_q[1].third()

    @pl.when(outer)
    def _():
        plane_o[0].rest()
        plane_q[3].third()

    def project_q(h):
        part_q[...] = jnp.zeros_like(part_q)

        @pl.loop(0, 8)
        def _(i):
            start = pl.multiple_of(i * shard, 16)
            part_q[...] += jnp.dot(
                turned[i], w_q[h, pl.ds(start, shard), :], preferred_element_type=jnp.float32)

        for g in range(2):
            q[:, g * 128:(g + 1) * 128] = head(part_q[:, g * 128:(g + 1) * 128], gain_q[...])

    def attend_head(h):
        @pl.loop(0, 2)
        def _(tile):
            first = pl.multiple_of(tile * half, half)
            keys = kv[pl.ds(first, span), h * 256:h * 256 + 128]
            values = kv[pl.ds(first, span), h * 256 + 128:h * 256 + 256]
            for g in range(2):
                cols = slice(g * 128, (g + 1) * 128)
                scores = lax.dot_general(
                    q[pl.ds(first, half), cols], keys, (((1,), (1,)), ((), ())),
                    preferred_element_type=jnp.float32)
                scores = scores + mask[tile]
                top = jnp.max(scores, axis=-1, keepdims=True)
                weights = jnp.exp2((scores - top) * (query_scale * LOG2_E))
                inverse = 1.0 / jnp.sum(weights, axis=-1, keepdims=True)
                weights = (weights * inverse).astype(jnp.bfloat16)
                cols = slice((2 * h + g) * 128, (2 * h + g + 1) * 128)
                mixed[at.z, pl.ds(first, half), cols] = jnp.dot(
                    weights, values, preferred_element_type=jnp.float32).astype(jnp.bfloat16)

    def relay_inner(h):
        @pl.when(at.z == 1)
        def _():
            line_m.falling(1, h)

        @pl.when(at.z == 2)
        def _():
            line_m.rising(1, h)

    def relay_outer(s, h):
        @pl.when(at.z == (1 if s == 1 else 2))
        def _():
            line_m.rising(s, h)

        @pl.when(at.z == (2 if s == 1 else 1))
        def _():
            line_m.falling(s, h)

    for h in range(heads):
        project_q(h)
        if h == 0:
            @pl.when(outer)
            def _():
                plane_o[0].first()
                plane_o[1].begin()
                plane_o[1].rest()
        halo.need(h)
        attend_head(h)
        line_m.start(h)

        @pl.when(inner)
        def _():
            if h == 1:
                relay_inner(0)
                plane_q[2].first()
                plane_q[3].start()
                plane_q[2].second()
                relay_inner(1)
                plane_q[2].third()
            if h == 2:
                plane_q[3].first()
                plane_o[0].start()
                plane_q[3].second()
                relay_inner(2)
                plane_q[3].third()
            if h == 3:
                plane_o[0].first()
                plane_o[1].start()
                relay_inner(3)

    def output(tile, p):
        some = pl.ds(tile * wide, wide)

        def step(j, _):
            total_o[some, :] += lax.dot_general(
                o_all[j * 2 + p, some, :], mixed[j, :, p * (nq // 2):(p + 1) * (nq // 2)],
                (((1,), (1,)), ((), ())), preferred_element_type=jnp.float32)
        return step

    last = jnp.where(at.z < 2, 3, 0)

    @pl.when(inner)
    def _():
        relay_outer(1, 0)
        relay_outer(1, 1)
        relay_outer(2, 0)
        plane_o[0].second()
        relay_outer(1, 2)
        relay_outer(2, 1)
        plane_o[0].third()
        relay_outer(1, 3)
        relay_outer(2, 2)
        plane_o[1].first()
        relay_outer(2, 3)

    @pl.when(outer)
    def _():
        plane_o[0].second()
        plane_o[0].third()
        for s in (1, 2):
            for h in range(heads):
                line_m.step(s, h)
        plane_o[1].first()

    for p in range(2):
        each(lambda j: j != last, (0,), output(0, p))
    plane_o[1].second()
    plane_o[1].third()
    for p in range(2):
        each(lambda j: j != last, (0,), output(1, p))
    line_m.step(3, 0)
    line_m.step(3, 1)
    each(lambda j: j == last, (0,), output(0, 0), output(1, 0))
    line_m.step(3, 2)
    line_m.step(3, 3)
    for tile in range(2):
        some = pl.ds(tile * wide, wide)
        rest = lax.dot_general(
            o_all[last * 2 + 1, some, :], mixed[last, :, nq // 2:],
            (((1,), (1,)), ((), ())), preferred_element_type=jnp.float32)
        out[some, :] = (total_o[some, :] + rest).astype(jnp.bfloat16)
    line.finish()
    line_m.finish()
    for plane in [plane_k] + plane_q + plane_o:
        plane.finish()
    halo.finish()


def fused(tokens, w_query, key_weight, value_weight, w_output, query_gain, key_gain):
    rows, depth = tokens.shape
    nq, nk = w_query.shape[1], key_weight.shape[1]
    features = w_output.shape[1]
    freqs = 10000.0 ** (-(jnp.arange(64, dtype=jnp.float32) * 2.0 / HEAD_SIZE))
    freqs = freqs.reshape(1, HEAD_SIZE // 2)
    hbm = pl.BlockSpec(memory_space=pl.ANY)
    vmem = pl.BlockSpec(memory_space=pltpu.VMEM)
    bf16, dma = jnp.bfloat16, pltpu.SemaphoreType.DMA
    return pl.pallas_call(
        kernel,
        out_shape=jax.ShapeDtypeStruct((features, rows), bf16),
        in_specs=[hbm] * 8,
        out_specs=vmem,
        scratch_shapes=[
            pltpu.VMEM((4, depth, rows), bf16),
            pltpu.VMEM((8, rows, depth // 2), bf16),
            pltpu.VMEM((4 * depth, 2 * nk), bf16),
            pltpu.VMEM((nq // 256, 4 * depth, 256), bf16),
            pltpu.VMEM((rows, 2 * nk), jnp.float32),
            pltpu.VMEM((rows, 256), jnp.float32),
            pltpu.VMEM((8, features, nq // 2), bf16),
            pltpu.VMEM((4, rows, nq), bf16),
            pltpu.VMEM((3 * rows, 2 * nk), bf16),
            pltpu.VMEM((rows, 256), bf16),
            pltpu.VMEM((features, rows), jnp.float32),
            pltpu.VMEM((2, rows // 2, rows // 2 + WINDOW_KEYS), jnp.float32),
            pltpu.VMEM((rows, HEAD_SIZE), jnp.float32),
            pltpu.VMEM((rows, HEAD_SIZE), jnp.float32),
            pltpu.VMEM((1, HEAD_SIZE), jnp.float32),
            pltpu.VMEM((1, HEAD_SIZE), jnp.float32),
            pltpu.VMEM((1, HEAD_SIZE // 2), jnp.float32),
            dma((2,)), dma((4, 2)), dma((1,)), dma((5,)), dma((4, 1)), dma((4, 5)),
            dma((2,)), dma((4, 4)), dma((2, 1)), dma((2, 5)), dma((2,)), dma((2, 4)), dma((8,)),
        ],
        compiler_params=pltpu.CompilerParams(
            collective_id=0, has_side_effects=True, vmem_limit_bytes=62 * MIB),
    )(tokens.T, w_query, key_weight, value_weight, w_output.T,
      query_gain.reshape(1, HEAD_SIZE), key_gain.reshape(1, HEAD_SIZE), freqs).T


def solution(mesh):
    small = dict(mesh.shape) == {"seq": 2, "row": 4, "col": 4}
    split = P(("seq", "row"), "col")
    return jax.shard_map(
        fused if small else shards,
        mesh=mesh,
        in_specs=(split, split, split, split, split, P(), P()),
        out_specs=split,
        check_vma=False,
    )
```

```python
import jax
import jax.numpy as jnp
from jax import lax
from jax.experimental import pallas as pl
from jax.experimental.pallas import tpu as pltpu
from jax.sharding import PartitionSpec as P

HEAD_SIZE = 128
WINDOW_KEYS = 1024


query_scale = 168.0 ** (-0.5)


def shifted(block, axis, distance):
    devices = range(lax.axis_size(axis))
    route = [(i - distance, i) for i in devices if i - distance in devices]
    return lax.ppermute(block, axis, route)


def head_norm(block, gain):
    mean_square = jnp.mean(block * block, axis=-1, keepdims=True)
    return block * lax.rsqrt(mean_square + 1e-06) * gain


def rotate(block, positions):
    half = block.shape[-1] // 2
    freqs = 10000.0 ** (-(jnp.arange(half, dtype=jnp.float32) * 2.0 / block.shape[-1]))
    angles = positions.astype(jnp.float32)[:, None] * freqs[None, :]
    cosine = jnp.cos(angles)[:, None, :]
    sine = jnp.sin(angles)[:, None, :]
    first = block[..., :half]
    second = block[..., half:]
    return jnp.concatenate(
        [first * cosine - second * sine, second * cosine + first * sine], axis=-1
    )


def attend(queries, key_states, value_states, qpos, kpos):
    rows = queries.shape[0]
    kv_heads = key_states.shape[1]
    grouped = queries.reshape(rows, kv_heads, 2, HEAD_SIZE)
    scores = (
        jnp.einsum("bhgd,khd->hgbk", grouped, key_states, preferred_element_type=jnp.float32)
        * query_scale
    )
    gap = qpos[:, None] - kpos[None, :]
    valid = (kpos[None, :] >= 0) & (gap >= 0) & (gap < WINDOW_KEYS)
    scores = jnp.where(valid[None, None], scores, -1e30)
    top = jnp.max(scores, axis=-1, keepdims=True)
    weights = jnp.exp(scores - top)
    weights = (weights / jnp.sum(weights, axis=-1, keepdims=True)).astype(jnp.bfloat16)
    mixed = jnp.einsum("hgbk,khd->bhgd", weights, value_states, preferred_element_type=jnp.float32)
    return mixed.astype(jnp.bfloat16).reshape(rows, kv_heads * 2 * HEAD_SIZE)


def shards(tokens, w_query, key_weight, value_weight, w_output, query_gain, key_gain):
    rows = tokens.shape[0]
    whole = lax.all_gather(tokens, "col", axis=1, tiled=True)
    columns = whole
    proj_q = jnp.dot(
        columns,
        lax.all_gather(w_query, ("seq", "row"), axis=0, tiled=True),
        preferred_element_type=jnp.float32,
    )
    projected_key = jnp.dot(
        columns,
        lax.all_gather(key_weight, ("seq", "row"), axis=0, tiled=True),
        preferred_element_type=jnp.float32,
    )
    proj_v = jnp.dot(
        columns,
        lax.all_gather(value_weight, ("seq", "row"), axis=0, tiled=True),
        preferred_element_type=jnp.float32,
    )
    base = lax.axis_index(("seq", "row")) * rows
    positions = base + jnp.arange(rows, dtype=jnp.int32)
    q_heads = proj_q.shape[1] // HEAD_SIZE
    kv_heads = projected_key.shape[1] // HEAD_SIZE
    queries = rotate(
        head_norm(proj_q.reshape(rows, q_heads, HEAD_SIZE), query_gain), positions
    ).astype(jnp.bfloat16)
    key_states = rotate(
        head_norm(projected_key.reshape(rows, kv_heads, HEAD_SIZE), key_gain), positions
    ).astype(jnp.bfloat16)
    key_flat = key_states.reshape(rows, kv_heads * HEAD_SIZE)
    value_flat = proj_v.astype(jnp.bfloat16)
    prior_one = shifted((key_flat, value_flat), ("seq", "row"), 1)
    prior_two = shifted((key_flat, value_flat), ("seq", "row"), 2)
    key_rows = jnp.concatenate([prior_two[0], prior_one[0], key_flat], axis=0).reshape(
        3 * rows, kv_heads, HEAD_SIZE
    )
    value_rows = jnp.concatenate([prior_two[1], prior_one[1], value_flat], axis=0).reshape(
        3 * rows, kv_heads, HEAD_SIZE
    )
    kpos = base - 2 * rows + jnp.arange(3 * rows, dtype=jnp.int32)
    mixed = attend(queries, key_rows, value_rows, positions, kpos)
    all_heads = lax.all_gather(mixed, "col", axis=1, tiled=True)
    columns = all_heads
    attended = jnp.dot(
        columns,
        lax.all_gather(w_output, ("seq", "row"), axis=0, tiled=True),
        preferred_element_type=jnp.float32,
    )
    return attended.astype(jnp.bfloat16)


MESH = pl.DeviceIdType.MESH
MIB = 1 << 20
LOG2_E = 1.4426950408889634


class Place:
    def __init__(self):
        self.y = lax.axis_index("seq")
        row = lax.axis_index("row")
        self.x, self.c = row // 2, row % 2
        self.z = lax.axis_index("col")
        self.to_x = {"seq": self.y, "row": (1 - self.x) * 2 + self.c, "col": self.z}
        self.to_y = {"seq": 1 - self.y, "row": row, "col": self.z}
        self.to_c = {"seq": self.y, "row": self.x * 2 + 1 - self.c, "col": self.z}
        self.up = {"seq": self.y, "row": row, "col": self.z + 1}
        self.down = {"seq": self.y, "row": row, "col": self.z - 1}
        self.to_d = {"seq": 1 - self.y, "row": (1 - self.x) * 2 + self.c, "col": self.z}
        self.chip = self.y * 2 + self.x
        after = (self.chip + 1) % 4
        self.after = {"seq": after // 2, "row": (after % 2) * 2 + self.c, "col": self.z}
        self.chip_x = self.y * 2 + 1 - self.x
        self.chip_y = (1 - self.y) * 2 + self.x
        self.chip_d = (1 - self.y) * 2 + 1 - self.x


def barrier(at):
    sem = pltpu.get_barrier_semaphore()
    for device in (at.to_x, at.to_y, at.to_c, at.to_d):
        pl.semaphore_signal(sem, inc=1, device_id=device, device_id_type=MESH)

    @pl.when(at.z < 3)
    def _():
        pl.semaphore_signal(sem, inc=1, device_id=at.up, device_id_type=MESH)

    @pl.when(at.z > 0)
    def _():
        pl.semaphore_signal(sem, inc=1, device_id=at.down, device_id_type=MESH)

    peers = 4 + (at.z < 3).astype(jnp.int32) + (at.z > 0).astype(jnp.int32)
    pl.semaphore_wait(sem, peers)


class Line:
    def __init__(self, at, whole, part, send, recv):
        self.at, self.whole, self.part, self.send, self.recv = at, whole, part, send, recv

    def copy(self, block, part, way):
        piece = self.part(block, part)
        return pltpu.make_async_remote_copy(
            src_ref=piece, dst_ref=piece,
            send_sem=self.send.at[way], recv_sem=self.recv.at[block, part],
            device_id=self.at.up if way == 0 else self.at.down, device_id_type=MESH)

    def start(self, part):
        at = self.at

        @pl.when(at.z < 3)
        def _():
            self.copy(at.z, part, 0).start()

        @pl.when(at.z > 0)
        def _():
            self.copy(at.z, part, 1).start()

    def rising(self, s, part):
        at = self.at

        @pl.when(at.z - s >= 0)
        def _():
            self.copy(at.z - s, part, 0).wait_recv()

            @pl.when(at.z < 3)
            def _():
                self.copy(at.z - s, part, 0).start()

    def falling(self, s, part):
        at = self.at

        @pl.when(at.z + s <= 3)
        def _():
            self.copy(at.z + s, part, 1).wait_recv()

            @pl.when(at.z > 0)
            def _():
                self.copy(at.z + s, part, 1).start()

    def step(self, s, part):
        self.rising(s, part)
        self.falling(s, part)

    def sent(self, way, blocks):
        piece = self.whole.at[pl.ds(0, blocks)]
        pltpu.make_async_remote_copy(
            src_ref=piece, dst_ref=piece,
            send_sem=self.send.at[way], recv_sem=self.recv.at[0, 0],
            device_id=self.at.up if way == 0 else self.at.down, device_id_type=MESH).wait_send()

    def finish(self):
        for z in range(4):
            @pl.when(self.at.z == z)
            def _():
                if z < 3:
                    self.sent(0, z + 1)
                if z > 0:
                    self.sent(1, 4 - z)


class Plane:
    def __init__(self, at, shards, cut, send, recv):
        self.at, self.shards, self.cut, self.send, self.recv = at, shards, cut, send, recv

    def copy(self, piece, device, slot):
        return pltpu.make_async_remote_copy(
            src_ref=piece, dst_ref=piece, send_sem=self.send.at[0],
            recv_sem=self.recv.at[slot], device_id=device, device_id_type=MESH)

    def half(self, chip, h):
        return self.cut(chip * 2 + self.at.c, h)

    def push(self, chip, h, device, slot):
        self.copy(self.half(chip, h), device, slot).start()

    def share(self, chip, slot=4):
        self.copy(self.shards(chip * 2 + self.at.c, 1), self.at.to_c, slot).start()

    def need(self, piece, slot):
        self.copy(piece, self.at.to_c, slot).wait_recv()

    def begin(self):
        at = self.at
        self.push(at.chip, 0, at.to_x, 0)
        self.push(at.chip, 1, at.to_y, 1)
        self.share(at.chip)

    def rest(self):
        at = self.at
        self.push(at.chip, 1, at.to_x, 2)
        self.push(at.chip, 0, at.to_y, 2)

    def start(self):
        self.begin()
        self.rest()

    def first(self):
        at = self.at
        self.need(self.half(at.chip_x, 0), 0)
        self.push(at.chip_x, 0, at.to_y, 3)
        self.need(self.half(at.chip_y, 1), 1)
        self.push(at.chip_y, 1, at.to_x, 3)

    def second(self):
        at = self.at
        self.need(self.shards(0, 1), 2)
        self.share(at.chip_x)
        self.share(at.chip_y)

    def third(self):
        at = self.at
        self.need(self.shards(0, 1), 3)
        self.share(at.chip_d, 5)
        self.need(self.shards(0, 1), 5)

    def sister(self):
        self.need(self.shards(0, 3), 4)

    def last(self):
        self.third()
        self.sister()

    def finish(self):
        self.copy(self.shards(0, 7), self.at.to_c, 0).wait_send()


class Halo:
    def __init__(self, at, kv, rows, send, recv):
        self.at, self.kv, self.rows, self.send, self.recv = at, kv, rows, send, recv

    def piece(self, block, h):
        cols = pl.ds(pl.multiple_of(h * 256, 256), 256)
        return self.kv.at[pl.ds(block * self.rows, self.rows), cols]

    def on(self, h):
        return pltpu.make_async_remote_copy(
            src_ref=self.piece(2, h), dst_ref=self.piece(0, h),
            send_sem=self.send.at[0], recv_sem=self.recv.at[0, h],
            device_id=self.at.after, device_id_type=MESH)

    def across(self, block, h):
        return pltpu.make_async_remote_copy(
            src_ref=self.piece(block, h), dst_ref=self.piece(1, h),
            send_sem=self.send.at[1], recv_sem=self.recv.at[1, h],
            device_id=self.at.to_c, device_id_type=MESH)

    def start(self, h):
        @pl.when(self.at.chip < 3)
        def _():
            self.on(h).start()

        @pl.when(self.at.c == 0)
        def _():
            self.across(2, h).start()

    def need(self, h):
        at = self.at

        @pl.when(at.chip > 0)
        def _():
            self.on(h).wait_recv()

            @pl.when(at.c == 1)
            def _():
                self.across(0, h).start()

        @pl.when((at.chip > 0) | (at.c == 1))
        def _():
            self.across(0, h).wait_recv()

    def sent(self, way):
        block = self.kv.at[pl.ds(0, self.rows)]
        pltpu.make_async_remote_copy(
            src_ref=block, dst_ref=block, send_sem=self.send.at[way],
            recv_sem=self.recv.at[0, 0], device_id=self.at.to_c, device_id_type=MESH).wait_send()

    def finish(self):
        at = self.at

        @pl.when(at.chip < 3)
        def _():
            self.sent(0)

        @pl.when((at.chip > 0) | (at.c == 0))
        def _():
            self.sent(1)


def kernel(x, wq, wk, wv, wo, query_gain, key_gain, freqs, out,
           x_all, turned, w_kv, w_q, total, o_all, mixed, kv, total_o, mask, result,
           cosine, sine, gain_q, gain_k, steps,
           zs, zr, ks, kr, qs, qr, ms, mr, os, orr, hs, hr, local):
    at = Place()
    depth, rows = x.shape
    nq, nk = wq.shape[1], wk.shape[1]
    features = wo.shape[0]
    heads = nk // 128
    shard = depth // 2
    device = at.chip * 2 + at.c
    outer = (at.z == 0) | (at.z == 3)
    inner = jnp.logical_not(outer)
    mine = pl.ds(pl.multiple_of(device * shard, 16), shard)
    load_x = pltpu.make_async_copy(x, x_all.at[at.z], local.at[0])
    load_kv = [
        pltpu.make_async_copy(wk, w_kv.at[mine, pl.ds(0, nk)], local.at[1]),
        pltpu.make_async_copy(wv, w_kv.at[mine, pl.ds(nk, nk)], local.at[2]),
    ]
    load_q = [
        pltpu.make_async_copy(wq.at[:, pl.ds(h * 256, 256)], w_q.at[h, mine], local.at[3])
        for h in range(heads)
    ]
    loads_q = pltpu.make_async_copy(w_q.at[:, mine], w_q.at[:, mine], local.at[3])
    load_o = pltpu.make_async_copy(wo, o_all.at[device], local.at[4])
    load_small = [
        pltpu.make_async_copy(query_gain, gain_q, local.at[5]),
        pltpu.make_async_copy(key_gain, gain_k, local.at[6]),
        pltpu.make_async_copy(freqs, steps, local.at[7]),
    ]
    for load in [load_x] + load_kv + load_q + load_small:
        load.start()
    barrier(at)
    half = rows // 2
    wide = features // 2

    def kv_cut(index, h):
        start = pl.multiple_of(index * shard + h * (shard // 2), 16)
        return w_kv.at[pl.ds(start, shard // 2)]

    def kv_shards(index, n):
        return w_kv.at[pl.ds(pl.multiple_of(index * shard, 16), n * shard)]

    def q_cut(head):
        def piece(index, h):
            start = pl.multiple_of(index * shard + h * (shard // 2), 16)
            return w_q.at[head, pl.ds(start, shard // 2)]
        return piece

    def q_shards(head):
        def piece(index, n):
            return w_q.at[head, pl.ds(pl.multiple_of(index * shard, 16), n * shard)]
        return piece

    def o_cut(tile):
        def piece(index, h):
            return o_all.at[index, pl.ds(tile * wide + h * (wide // 2), wide // 2)]
        return piece

    def o_shards(tile):
        def piece(index, n):
            return o_all.at[pl.ds(index, n), pl.ds(tile * wide, wide)]
        return piece

    line = Line(at, x_all, lambda b, p: x_all.at[b, pl.ds(p * shard, shard)], zs, zr)
    line_m = Line(at, mixed, lambda b, p: mixed.at[b, :, pl.ds(p * 256, 256)], ms, mr)
    plane_k = Plane(at, kv_shards, kv_cut, ks, kr)
    plane_q = [Plane(at, q_shards(h), q_cut(h), qs.at[h], qr.at[h]) for h in range(heads)]
    plane_o = [Plane(at, o_shards(t), o_cut(t), os.at[t], orr.at[t]) for t in range(2)]
    halo = Halo(at, kv, rows, hs, hr)

    def apart(distance):
        return lambda j: (j - at.z == distance) | (at.z - j == distance)

    def project(j, p):
        start = pl.multiple_of((j * 2 + p) * shard, 16)
        total[...] += jnp.dot(
            turned[j * 2 + p], w_kv[pl.ds(start, shard), :], preferred_element_type=jnp.float32)

    def each(which, parts, *steps):
        @pl.loop(0, 4)
        def _(j):
            @pl.when(which(j))
            def _():
                for p in parts:
                    for step in steps:
                        step(j, p)

    def turn(j, p):
        turned[j * 2 + p] = x_all[j, p * shard:(p + 1) * shard, :].T

    load_x.wait()
    line.start(0)
    for load in load_kv:
        load.wait()
    plane_k.start()
    line.start(1)
    load_o.start()
    turn(at.z, 0)
    turn(at.z, 1)
    total[...] = jnp.zeros_like(total)
    total_o[...] = jnp.zeros_like(total_o)

    @pl.when(at.chip == 0)
    def _():
        kv[pl.ds(0, rows), :] = jnp.zeros((rows, 2 * nk), jnp.bfloat16)

        @pl.when(at.c == 0)
        def _():
            kv[pl.ds(rows, rows), :] = jnp.zeros((rows, 2 * nk), jnp.bfloat16)

    loads_q.wait()
    load_o.wait()
    for load in load_small:
        load.wait()

    plane_k.first()
    plane_q[0].start()
    plane_q[1].start()
    line.step(1, 0)

    positions = device * rows + lax.broadcasted_iota(jnp.int32, (rows, 128), 0)
    angles = positions.astype(jnp.float32) * jnp.concatenate([steps[...], steps[...]], axis=1)
    lower = lax.broadcasted_iota(jnp.int32, (rows, 128), 1) < 64
    cosine[...] = jnp.cos(angles)
    turned_sine = jnp.sin(angles)
    sine[...] = jnp.where(lower, -turned_sine, turned_sine)

    span = half + 2 * rows
    for tile in range(2):
        query = lax.broadcasted_iota(jnp.int32, (half, span), 0)
        key = lax.broadcasted_iota(jnp.int32, (half, span), 1)
        low = 2 * rows - device * rows - tile * half
        valid = (key > query) & (key <= query + WINDOW_KEYS) & (key >= low)
        mask[tile] = jnp.where(valid, 0.0, -1e30)

    each(apart(1), (0,), turn)
    plane_k.second()
    line.step(1, 1)
    each(apart(1), (1,), turn)
    line.step(2, 0)
    plane_k.last()
    each(apart(0), (0, 1), project)
    each(apart(1), (0, 1), project)
    plane_q[0].first()
    plane_q[0].second()
    each(apart(2), (0,), turn, project)
    line.step(2, 1)
    plane_q[1].first()

    @pl.when(outer)
    def _():
        plane_q[2].start()
        plane_q[3].start()

    each(apart(2), (1,), turn, project)
    plane_q[0].last()
    plane_q[1].second()

    @pl.when(outer)
    def _():
        plane_q[1].last()
        line.step(3, 0)

    each(apart(3), (0,), turn, project)

    @pl.when(outer)
    def _():
        plane_q[2].first()
        plane_q[2].second()
        plane_q[3].first()
        plane_o[0].begin()
        plane_q[3].second()
        plane_q[2].last()
        line.step(3, 1)

    each(apart(3), (1,), turn, project)

    def head(block, gain):
        mean_square = jnp.mean(block * block, axis=-1, keepdims=True)
        normed = block * lax.rsqrt(mean_square + 1e-06) * gain
        spun = normed * cosine[...] + pltpu.roll(normed, 64, 1) * sine[...]
        return spun.astype(jnp.bfloat16)

    own = pl.ds(2 * rows, rows)

    @pl.loop(0, heads)
    def _(h):
        keys = total[:, pl.ds(pl.multiple_of(h * 128, 128), 128)]
        kv[own, pl.ds(pl.multiple_of(h * 256, 256), 128)] = head(keys, gain_k[...])
        values = total[:, pl.ds(pl.multiple_of(nk + h * 128, 128), 128)]
        kv[own, pl.ds(pl.multiple_of(h * 256 + 128, 128), 128)] = values.astype(jnp.bfloat16)
        halo.start(h)

    @pl.when(inner)
    def _():
        plane_q[2].start()
        plane_q[1].last()

    @pl.when(outer)
    def _():
        plane_o[0].rest()
        plane_q[3].last()

    def project_q(h):
        cols = slice(h * 256, (h + 1) * 256)
        total[:, cols] = jnp.zeros((rows, 256), jnp.float32)

        @pl.loop(0, 2)
        def _(i):
            block = total[:, cols]
            for u in range(4):
                start = pl.multiple_of((i * 4 + u) * shard, 16)
                block += jnp.dot(
                    turned[i * 4 + u], w_q[h, pl.ds(start, shard), :],
                    preferred_element_type=jnp.float32)
            total[:, cols] = block

        for g in range(2 * h, 2 * h + 2):
            cols = slice(g * 128, (g + 1) * 128)
            mixed[at.z, :, cols] = head(total[:, cols], gain_q[...])

    def attend_head(h):
        @pl.loop(0, 2)
        def _(tile):
            first = pl.multiple_of(tile * half, half)
            keys = kv[pl.ds(first, span), h * 256:h * 256 + 128]
            values = kv[pl.ds(first, span), h * 256 + 128:h * 256 + 256]
            for g in range(2):
                cols = slice((2 * h + g) * 128, (2 * h + g + 1) * 128)
                scores = lax.dot_general(
                    mixed[at.z, pl.ds(first, half), cols], keys, (((1,), (1,)), ((), ())),
                    preferred_element_type=jnp.float32)
                scores = scores + mask[tile]
                top = jnp.max(scores, axis=-1, keepdims=True)
                weights = jnp.exp2((scores - top) * (query_scale * LOG2_E))
                inverse = 1.0 / jnp.sum(weights, axis=-1, keepdims=True)
                weights = (weights * inverse).astype(jnp.bfloat16)
                mixed[at.z, pl.ds(first, half), cols] = jnp.dot(
                    weights, values, preferred_element_type=jnp.float32).astype(jnp.bfloat16)

    def relay_inner(h):
        @pl.when(at.z == 1)
        def _():
            line_m.falling(1, h)

        @pl.when(at.z == 2)
        def _():
            line_m.rising(1, h)

    def relay_outer(s, h):
        @pl.when(at.z == (1 if s == 1 else 2))
        def _():
            line_m.rising(s, h)

        @pl.when(at.z == (2 if s == 1 else 1))
        def _():
            line_m.falling(s, h)

    project_q(0)
    project_q(1)

    @pl.when(outer)
    def _():
        plane_o[0].first()
        plane_o[1].start()

    for h in range(heads):
        if h > 1:
            project_q(h)
        halo.need(h)
        attend_head(h)
        line_m.start(h)

        @pl.when(inner)
        def _():
            if h == 1:
                relay_inner(0)
                plane_q[2].first()
                plane_q[3].start()
                plane_q[2].second()
                relay_inner(1)
                plane_q[2].last()
            if h == 2:
                plane_q[3].first()
                plane_o[0].start()
                plane_q[3].second()
                relay_inner(2)
                plane_q[3].last()
            if h == 3:
                plane_o[0].first()
                plane_o[1].start()
                relay_inner(3)

    def output(tile, p):
        some = pl.ds(tile * wide, wide)

        def step(j, _):
            total_o[some, :] += lax.dot_general(
                o_all[j * 2 + p, some, :], mixed[j, :, p * (nq // 2):(p + 1) * (nq // 2)],
                (((1,), (1,)), ((), ())), preferred_element_type=jnp.float32)
        return step

    last = jnp.where(at.z < 2, 3, 0)

    @pl.when(inner)
    def _():
        relay_outer(1, 0)
        relay_outer(1, 1)
        relay_outer(2, 0)
        plane_o[0].second()
        relay_outer(1, 2)
        relay_outer(2, 1)
        plane_o[0].last()
        relay_outer(1, 3)
        relay_outer(2, 2)
        plane_o[1].first()
        relay_outer(2, 3)

    @pl.when(outer)
    def _():
        plane_o[0].second()
        plane_o[0].last()
        for s in (1, 2):
            for h in range(heads):
                line_m.step(s, h)
        plane_o[1].first()

    def store(tile):
        some = pl.ds(tile * wide, wide)
        result[some, :] = total_o[some, :].astype(jnp.bfloat16)
        one = pltpu.make_async_copy(result.at[some], out.at[some], local.at[8 + tile])
        one.start()
        return one

    for p in range(2):
        each(lambda j: j != last, (0,), output(0, p))

    plane_o[1].second()
    plane_o[1].sister()
    for p in range(2):
        each(lambda j: (j != at.chip_d) & (inner | (j != last)), (0,), output(1, p))

    def final(p):
        line_m.step(3, 2 * p)
        line_m.step(3, 2 * p + 1)
        each(lambda j: j == last, (0,), output(0, p))
        each(lambda j: outer & (j == last) & (j != at.chip_d), (0,), output(1, p))

    final(0)

    @pl.when(outer)
    def _():
        plane_o[1].third()

    each(lambda j: (j == at.chip_d) & outer, (0,), output(1, 0))
    each(lambda j: (j == at.chip_d) & outer & (j != last), (0,), output(1, 1))
    final(1)
    stores = [store(0)]

    @pl.when(inner)
    def _():
        plane_o[1].third()

    each(lambda j: (j == at.chip_d) & inner, (0,), output(1, 0))
    each(lambda j: (j == at.chip_d) & (inner | (j == last)), (0,), output(1, 1))
    stores.append(store(1))
    line.finish()
    line_m.finish()
    for plane in [plane_k] + plane_q + plane_o:
        plane.finish()
    halo.finish()
    for one in stores:
        one.wait()


def fused(tokens, w_query, key_weight, value_weight, w_output, query_gain, key_gain):
    rows, depth = tokens.shape
    nq, nk = w_query.shape[1], key_weight.shape[1]
    features = w_output.shape[1]
    freqs = 10000.0 ** (-(jnp.arange(64, dtype=jnp.float32) * 2.0 / HEAD_SIZE))
    freqs = freqs.reshape(1, HEAD_SIZE // 2)
    hbm = pl.BlockSpec(memory_space=pl.ANY)
    bf16, dma = jnp.bfloat16, pltpu.SemaphoreType.DMA
    return pl.pallas_call(
        kernel,
        out_shape=jax.ShapeDtypeStruct((features, rows), bf16),
        in_specs=[hbm] * 8,
        out_specs=hbm,
        scratch_shapes=[
            pltpu.VMEM((4, depth, rows), bf16),
            pltpu.VMEM((8, rows, depth // 2), bf16),
            pltpu.VMEM((4 * depth, 2 * nk), bf16),
            pltpu.VMEM((nq // 256, 4 * depth, 256), bf16),
            pltpu.VMEM((rows, 2 * nk), jnp.float32),
            pltpu.VMEM((8, features, nq // 2), bf16),
            pltpu.VMEM((4, rows, nq), bf16),
            pltpu.VMEM((3 * rows, 2 * nk), bf16),
            pltpu.VMEM((features, rows), jnp.float32),
            pltpu.VMEM((2, rows // 2, rows // 2 + WINDOW_KEYS), jnp.float32),
            pltpu.VMEM((features, rows), bf16),
            pltpu.VMEM((rows, HEAD_SIZE), jnp.float32),
            pltpu.VMEM((rows, HEAD_SIZE), jnp.float32),
            pltpu.VMEM((1, HEAD_SIZE), jnp.float32),
            pltpu.VMEM((1, HEAD_SIZE), jnp.float32),
            pltpu.VMEM((1, HEAD_SIZE // 2), jnp.float32),
            dma((2,)), dma((4, 2)), dma((1,)), dma((6,)), dma((4, 1)), dma((4, 6)),
            dma((2,)), dma((4, 4)), dma((2, 1)), dma((2, 6)), dma((2,)), dma((2, 4)), dma((10,)),
        ],
        compiler_params=pltpu.CompilerParams(
            collective_id=0, has_side_effects=True, vmem_limit_bytes=62 * MIB),
    )(tokens.T, w_query, key_weight, value_weight, w_output.T,
      query_gain.reshape(1, HEAD_SIZE), key_gain.reshape(1, HEAD_SIZE), freqs).T


def solution(mesh):
    small = dict(mesh.shape) == {"seq": 2, "row": 4, "col": 4}
    split = P(("seq", "row"), "col")
    return jax.shard_map(
        fused if small else shards,
        mesh=mesh,
        in_specs=(split, split, split, split, split, P(), P()),
        out_specs=split,
        check_vma=False,
    )
```

```python
import jax
import jax.numpy as jnp
from jax import lax
from jax.experimental import pallas as pl
from jax.experimental.pallas import tpu as pltpu
from jax.sharding import PartitionSpec as P

HEAD_SIZE = 128
WINDOW_KEYS = 1024


query_scale = 168.0 ** (-0.5)


def shifted(block, axis, distance):
    devices = range(lax.axis_size(axis))
    route = [(i - distance, i) for i in devices if i - distance in devices]
    return lax.ppermute(block, axis, route)


def head_norm(block, gain):
    mean_square = jnp.mean(block * block, axis=-1, keepdims=True)
    return block * lax.rsqrt(mean_square + 1e-06) * gain


def rotate(block, positions):
    half = block.shape[-1] // 2
    freqs = 10000.0 ** (-(jnp.arange(half, dtype=jnp.float32) * 2.0 / block.shape[-1]))
    angles = positions.astype(jnp.float32)[:, None] * freqs[None, :]
    cosine = jnp.cos(angles)[:, None, :]
    sine = jnp.sin(angles)[:, None, :]
    first = block[..., :half]
    second = block[..., half:]
    return jnp.concatenate(
        [first * cosine - second * sine, second * cosine + first * sine], axis=-1
    )


def attend(queries, key_states, value_states, qpos, kpos):
    rows = queries.shape[0]
    kv_heads = key_states.shape[1]
    grouped = queries.reshape(rows, kv_heads, 2, HEAD_SIZE)
    scores = (
        jnp.einsum("bhgd,khd->hgbk", grouped, key_states, preferred_element_type=jnp.float32)
        * query_scale
    )
    gap = qpos[:, None] - kpos[None, :]
    valid = (kpos[None, :] >= 0) & (gap >= 0) & (gap < WINDOW_KEYS)
    scores = jnp.where(valid[None, None], scores, -1e30)
    top = jnp.max(scores, axis=-1, keepdims=True)
    weights = jnp.exp(scores - top)
    weights = (weights / jnp.sum(weights, axis=-1, keepdims=True)).astype(jnp.bfloat16)
    mixed = jnp.einsum("hgbk,khd->bhgd", weights, value_states, preferred_element_type=jnp.float32)
    return mixed.astype(jnp.bfloat16).reshape(rows, kv_heads * 2 * HEAD_SIZE)


def shards(tokens, w_query, key_weight, value_weight, w_output, query_gain, key_gain):
    rows = tokens.shape[0]
    whole = lax.all_gather(tokens, "col", axis=1, tiled=True)
    columns = whole
    proj_q = jnp.dot(
        columns,
        lax.all_gather(w_query, ("seq", "row"), axis=0, tiled=True),
        preferred_element_type=jnp.float32,
    )
    projected_key = jnp.dot(
        columns,
        lax.all_gather(key_weight, ("seq", "row"), axis=0, tiled=True),
        preferred_element_type=jnp.float32,
    )
    proj_v = jnp.dot(
        columns,
        lax.all_gather(value_weight, ("seq", "row"), axis=0, tiled=True),
        preferred_element_type=jnp.float32,
    )
    base = lax.axis_index(("seq", "row")) * rows
    positions = base + jnp.arange(rows, dtype=jnp.int32)
    q_heads = proj_q.shape[1] // HEAD_SIZE
    kv_heads = projected_key.shape[1] // HEAD_SIZE
    queries = rotate(
        head_norm(proj_q.reshape(rows, q_heads, HEAD_SIZE), query_gain), positions
    ).astype(jnp.bfloat16)
    key_states = rotate(
        head_norm(projected_key.reshape(rows, kv_heads, HEAD_SIZE), key_gain), positions
    ).astype(jnp.bfloat16)
    key_flat = key_states.reshape(rows, kv_heads * HEAD_SIZE)
    value_flat = proj_v.astype(jnp.bfloat16)
    prior_one = shifted((key_flat, value_flat), ("seq", "row"), 1)
    prior_two = shifted((key_flat, value_flat), ("seq", "row"), 2)
    key_rows = jnp.concatenate([prior_two[0], prior_one[0], key_flat], axis=0).reshape(
        3 * rows, kv_heads, HEAD_SIZE
    )
    value_rows = jnp.concatenate([prior_two[1], prior_one[1], value_flat], axis=0).reshape(
        3 * rows, kv_heads, HEAD_SIZE
    )
    kpos = base - 2 * rows + jnp.arange(3 * rows, dtype=jnp.int32)
    mixed = attend(queries, key_rows, value_rows, positions, kpos)
    all_heads = lax.all_gather(mixed, "col", axis=1, tiled=True)
    columns = all_heads
    attended = jnp.dot(
        columns,
        lax.all_gather(w_output, ("seq", "row"), axis=0, tiled=True),
        preferred_element_type=jnp.float32,
    )
    return attended.astype(jnp.bfloat16)


MESH = pl.DeviceIdType.MESH
MIB = 1 << 20
LOG2_E = 1.4426950408889634


class Place:
    def __init__(self):
        self.y = lax.axis_index("seq")
        row = lax.axis_index("row")
        self.x, self.c = row // 2, row % 2
        self.z = lax.axis_index("col")
        self.to_x = {"seq": self.y, "row": (1 - self.x) * 2 + self.c, "col": self.z}
        self.to_y = {"seq": 1 - self.y, "row": row, "col": self.z}
        self.to_c = {"seq": self.y, "row": self.x * 2 + 1 - self.c, "col": self.z}
        self.up = {"seq": self.y, "row": row, "col": self.z + 1}
        self.down = {"seq": self.y, "row": row, "col": self.z - 1}
        self.to_d = {"seq": 1 - self.y, "row": (1 - self.x) * 2 + self.c, "col": self.z}
        self.chip = self.y * 2 + self.x
        after = (self.chip + 1) % 4
        self.after = {"seq": after // 2, "row": (after % 2) * 2 + self.c, "col": self.z}
        self.chip_x = self.y * 2 + 1 - self.x
        self.chip_y = (1 - self.y) * 2 + self.x
        self.chip_d = (1 - self.y) * 2 + 1 - self.x


def barrier(at):
    sem = pltpu.get_barrier_semaphore()
    for device in (at.to_x, at.to_y, at.to_c, at.to_d):
        pl.semaphore_signal(sem, inc=1, device_id=device, device_id_type=MESH)

    @pl.when(at.z < 3)
    def _():
        pl.semaphore_signal(sem, inc=1, device_id=at.up, device_id_type=MESH)

    @pl.when(at.z > 0)
    def _():
        pl.semaphore_signal(sem, inc=1, device_id=at.down, device_id_type=MESH)

    peers = 4 + (at.z < 3).astype(jnp.int32) + (at.z > 0).astype(jnp.int32)
    pl.semaphore_wait(sem, peers)


class Line:
    def __init__(self, at, whole, part, send, recv):
        self.at, self.whole, self.part, self.send, self.recv = at, whole, part, send, recv

    def copy(self, block, part, way):
        piece = self.part(block, part)
        return pltpu.make_async_remote_copy(
            src_ref=piece, dst_ref=piece,
            send_sem=self.send.at[way], recv_sem=self.recv.at[block, part],
            device_id=self.at.up if way == 0 else self.at.down, device_id_type=MESH)

    def start(self, part):
        at = self.at

        @pl.when(at.z < 3)
        def _():
            self.copy(at.z, part, 0).start()

        @pl.when(at.z > 0)
        def _():
            self.copy(at.z, part, 1).start()

    def rising(self, s, part):
        at = self.at

        @pl.when(at.z - s >= 0)
        def _():
            self.copy(at.z - s, part, 0).wait_recv()

            @pl.when(at.z < 3)
            def _():
                self.copy(at.z - s, part, 0).start()

    def falling(self, s, part):
        at = self.at

        @pl.when(at.z + s <= 3)
        def _():
            self.copy(at.z + s, part, 1).wait_recv()

            @pl.when(at.z > 0)
            def _():
                self.copy(at.z + s, part, 1).start()

    def step(self, s, part):
        self.rising(s, part)
        self.falling(s, part)

    def sent(self, way, blocks):
        piece = self.whole.at[pl.ds(0, blocks)]
        pltpu.make_async_remote_copy(
            src_ref=piece, dst_ref=piece,
            send_sem=self.send.at[way], recv_sem=self.recv.at[0, 0],
            device_id=self.at.up if way == 0 else self.at.down, device_id_type=MESH).wait_send()

    def finish(self):
        for z in range(4):
            @pl.when(self.at.z == z)
            def _():
                if z < 3:
                    self.sent(0, z + 1)
                if z > 0:
                    self.sent(1, 4 - z)


class Plane:
    def __init__(self, at, shards, cut, send, recv):
        self.at, self.shards, self.cut, self.send, self.recv = at, shards, cut, send, recv

    def copy(self, piece, device, slot):
        return pltpu.make_async_remote_copy(
            src_ref=piece, dst_ref=piece, send_sem=self.send.at[0],
            recv_sem=self.recv.at[slot], device_id=device, device_id_type=MESH)

    def half(self, chip, h):
        return self.cut(chip * 2 + self.at.c, h)

    def push(self, chip, h, device, slot):
        self.copy(self.half(chip, h), device, slot).start()

    def share(self, chip):
        self.copy(self.shards(chip * 2 + self.at.c, 1), self.at.to_c, 4).start()

    def need(self, piece, slot):
        self.copy(piece, self.at.to_c, slot).wait_recv()

    def begin(self):
        at = self.at
        self.push(at.chip, 0, at.to_x, 0)
        self.push(at.chip, 1, at.to_y, 1)
        self.share(at.chip)

    def rest(self):
        at = self.at
        self.push(at.chip, 1, at.to_x, 2)
        self.push(at.chip, 0, at.to_y, 2)

    def start(self):
        self.begin()
        self.rest()

    def first(self):
        at = self.at
        self.need(self.half(at.chip_x, 0), 0)
        self.push(at.chip_x, 0, at.to_y, 3)
        self.push(at.chip_x, 0, at.to_c, 4)
        self.need(self.half(at.chip_y, 1), 1)
        self.push(at.chip_y, 1, at.to_x, 6)
        self.push(at.chip_y, 1, at.to_c, 4)

    def second(self):
        at = self.at
        self.need(self.shards(0, 1), 2)
        self.push(at.chip_x, 1, at.to_c, 4)
        self.push(at.chip_y, 0, at.to_c, 4)

    def third(self):
        at = self.at
        self.need(self.half(at.chip_d, 0), 3)
        self.push(at.chip_d, 0, at.to_c, 5)
        self.need(self.half(at.chip_d, 1), 6)
        self.push(at.chip_d, 1, at.to_c, 5)
        self.need(self.shards(0, 1), 5)

    def sister(self):
        self.need(self.shards(0, 3), 4)

    def last(self):
        self.third()
        self.sister()

    def finish(self):
        self.copy(self.shards(0, 7), self.at.to_c, 0).wait_send()


class Halo:
    def __init__(self, at, kv, rows, send, recv):
        self.at, self.kv, self.rows, self.send, self.recv = at, kv, rows, send, recv

    def piece(self, block, h):
        cols = pl.ds(pl.multiple_of(h * 256, 256), 256)
        return self.kv.at[pl.ds(block * self.rows, self.rows), cols]

    def on(self, h):
        return pltpu.make_async_remote_copy(
            src_ref=self.piece(2, h), dst_ref=self.piece(0, h),
            send_sem=self.send.at[0], recv_sem=self.recv.at[0, h],
            device_id=self.at.after, device_id_type=MESH)

    def across(self, block, h):
        return pltpu.make_async_remote_copy(
            src_ref=self.piece(block, h), dst_ref=self.piece(1, h),
            send_sem=self.send.at[1], recv_sem=self.recv.at[1, h],
            device_id=self.at.to_c, device_id_type=MESH)

    def start(self, h):
        @pl.when(self.at.chip < 3)
        def _():
            self.on(h).start()

        @pl.when(self.at.c == 0)
        def _():
            self.across(2, h).start()

    def need(self, h):
        at = self.at

        @pl.when(at.chip > 0)
        def _():
            self.on(h).wait_recv()

            @pl.when(at.c == 1)
            def _():
                self.across(0, h).start()

        @pl.when((at.chip > 0) | (at.c == 1))
        def _():
            self.across(0, h).wait_recv()

    def sent(self, way):
        block = self.kv.at[pl.ds(0, self.rows)]
        pltpu.make_async_remote_copy(
            src_ref=block, dst_ref=block, send_sem=self.send.at[way],
            recv_sem=self.recv.at[0, 0], device_id=self.at.to_c, device_id_type=MESH).wait_send()

    def finish(self):
        at = self.at

        @pl.when(at.chip < 3)
        def _():
            self.sent(0)

        @pl.when((at.chip > 0) | (at.c == 0))
        def _():
            self.sent(1)


def kernel(x, wq, wk, wv, wo, query_gain, key_gain, freqs, out,
           x_all, turned, w_kv, w_q, total, o_all, mixed, kv, total_o, mask, result,
           cosine, sine, gain_q, gain_k, steps,
           zs, zr, ks, kr, qs, qr, ms, mr, os, orr, hs, hr, local):
    at = Place()
    depth, rows = x.shape
    nq, nk = wq.shape[1], wk.shape[1]
    features = wo.shape[0]
    heads = nk // 128
    shard = depth // 2
    device = at.chip * 2 + at.c
    outer = (at.z == 0) | (at.z == 3)
    inner = jnp.logical_not(outer)
    mine = pl.ds(pl.multiple_of(device * shard, 16), shard)
    load_x = pltpu.make_async_copy(x, x_all.at[at.z], local.at[0])
    load_kv = [
        pltpu.make_async_copy(wk, w_kv.at[mine, pl.ds(0, nk)], local.at[1]),
        pltpu.make_async_copy(wv, w_kv.at[mine, pl.ds(nk, nk)], local.at[2]),
    ]
    load_q = [
        pltpu.make_async_copy(wq.at[:, pl.ds(h * 256, 256)], w_q.at[h, mine], local.at[3])
        for h in range(heads)
    ]
    loads_q = pltpu.make_async_copy(w_q.at[:, mine], w_q.at[:, mine], local.at[3])
    load_o = pltpu.make_async_copy(wo, o_all.at[device], local.at[4])
    load_small = [
        pltpu.make_async_copy(query_gain, gain_q, local.at[5]),
        pltpu.make_async_copy(key_gain, gain_k, local.at[6]),
        pltpu.make_async_copy(freqs, steps, local.at[7]),
    ]
    for load in [load_x] + load_kv + load_q + load_small:
        load.start()
    barrier(at)
    half = rows // 2
    wide = features // 2

    def kv_cut(index, h):
        start = pl.multiple_of(index * shard + h * (shard // 2), 16)
        return w_kv.at[pl.ds(start, shard // 2)]

    def kv_shards(index, n):
        return w_kv.at[pl.ds(pl.multiple_of(index * shard, 16), n * shard)]

    def q_cut(head):
        def piece(index, h):
            start = pl.multiple_of(index * shard + h * (shard // 2), 16)
            return w_q.at[head, pl.ds(start, shard // 2)]
        return piece

    def q_shards(head):
        def piece(index, n):
            return w_q.at[head, pl.ds(pl.multiple_of(index * shard, 16), n * shard)]
        return piece

    def o_cut(tile):
        def piece(index, h):
            return o_all.at[index, pl.ds(tile * wide + h * (wide // 2), wide // 2)]
        return piece

    def o_shards(tile):
        def piece(index, n):
            return o_all.at[pl.ds(index, n), pl.ds(tile * wide, wide)]
        return piece

    line = Line(at, x_all, lambda b, p: x_all.at[b, pl.ds(p * shard, shard)], zs, zr)
    line_m = Line(at, mixed, lambda b, p: mixed.at[b, :, pl.ds(p * 256, 256)], ms, mr)
    plane_k = Plane(at, kv_shards, kv_cut, ks, kr)
    plane_q = [Plane(at, q_shards(h), q_cut(h), qs.at[h], qr.at[h]) for h in range(heads)]
    plane_o = [Plane(at, o_shards(t), o_cut(t), os.at[t], orr.at[t]) for t in range(2)]
    halo = Halo(at, kv, rows, hs, hr)

    def apart(distance):
        return lambda j: (j - at.z == distance) | (at.z - j == distance)

    def project(j, p):
        start = pl.multiple_of((j * 2 + p) * shard, 16)
        total[...] += jnp.dot(
            turned[j * 2 + p], w_kv[pl.ds(start, shard), :], preferred_element_type=jnp.float32)

    def each(which, parts, *steps):
        @pl.loop(0, 4)
        def _(j):
            @pl.when(which(j))
            def _():
                for p in parts:
                    for step in steps:
                        step(j, p)

    def turn(j, p):
        turned[j * 2 + p] = x_all[j, p * shard:(p + 1) * shard, :].T

    load_x.wait()
    line.start(0)
    for load in load_kv:
        load.wait()
    plane_k.start()
    line.start(1)
    load_o.start()
    turn(at.z, 0)
    turn(at.z, 1)
    total[...] = jnp.zeros_like(total)
    total_o[...] = jnp.zeros_like(total_o)

    @pl.when(at.chip == 0)
    def _():
        kv[pl.ds(0, rows), :] = jnp.zeros((rows, 2 * nk), jnp.bfloat16)

        @pl.when(at.c == 0)
        def _():
            kv[pl.ds(rows, rows), :] = jnp.zeros((rows, 2 * nk), jnp.bfloat16)

    loads_q.wait()
    load_o.wait()
    for load in load_small:
        load.wait()

    plane_k.first()
    plane_q[0].start()
    plane_q[1].start()
    line.step(1, 0)

    positions = device * rows + lax.broadcasted_iota(jnp.int32, (rows, 128), 0)
    angles = positions.astype(jnp.float32) * jnp.concatenate([steps[...], steps[...]], axis=1)
    lower = lax.broadcasted_iota(jnp.int32, (rows, 128), 1) < 64
    cosine[...] = jnp.cos(angles)
    turned_sine = jnp.sin(angles)
    sine[...] = jnp.where(lower, -turned_sine, turned_sine)

    span = half + 2 * rows
    for tile in range(2):
        query = lax.broadcasted_iota(jnp.int32, (half, span), 0)
        key = lax.broadcasted_iota(jnp.int32, (half, span), 1)
        low = 2 * rows - device * rows - tile * half
        valid = (key > query) & (key <= query + WINDOW_KEYS) & (key >= low)
        mask[tile] = jnp.where(valid, 0.0, -1e30)

    each(apart(1), (0,), turn)
    plane_k.second()
    line.step(1, 1)
    each(apart(1), (1,), turn)
    line.step(2, 0)
    plane_k.last()
    each(apart(0), (0, 1), project)
    each(apart(1), (0, 1), project)
    plane_q[0].first()
    plane_q[0].second()
    each(apart(2), (0,), turn, project)
    line.step(2, 1)
    plane_q[1].first()

    @pl.when(outer)
    def _():
        plane_q[2].start()
        plane_q[3].start()

    each(apart(2), (1,), turn, project)
    plane_q[0].last()
    plane_q[1].second()

    @pl.when(outer)
    def _():
        plane_q[1].last()
        line.step(3, 0)

    each(apart(3), (0,), turn, project)

    @pl.when(outer)
    def _():
        plane_q[2].first()
        plane_q[2].second()
        plane_q[3].first()
        plane_o[0].begin()
        plane_q[3].second()
        plane_q[2].last()
        line.step(3, 1)

    each(apart(3), (1,), turn, project)

    def head(block, gain):
        mean_square = jnp.mean(block * block, axis=-1, keepdims=True)
        normed = block * lax.rsqrt(mean_square + 1e-06) * gain
        spun = normed * cosine[...] + pltpu.roll(normed, 64, 1) * sine[...]
        return spun.astype(jnp.bfloat16)

    own = pl.ds(2 * rows, rows)

    @pl.loop(0, heads)
    def _(h):
        keys = total[:, pl.ds(pl.multiple_of(h * 128, 128), 128)]
        kv[own, pl.ds(pl.multiple_of(h * 256, 256), 128)] = head(keys, gain_k[...])
        values = total[:, pl.ds(pl.multiple_of(nk + h * 128, 128), 128)]
        kv[own, pl.ds(pl.multiple_of(h * 256 + 128, 128), 128)] = values.astype(jnp.bfloat16)
        halo.start(h)

    @pl.when(inner)
    def _():
        plane_q[2].start()
        plane_q[1].last()

    @pl.when(outer)
    def _():
        plane_o[0].rest()
        plane_o[1].start()
        plane_q[3].last()

    def project_q(h):
        cols = slice(h * 256, (h + 1) * 256)
        total[:, cols] = jnp.zeros((rows, 256), jnp.float32)

        @pl.loop(0, 2)
        def _(i):
            block = total[:, cols]
            for u in range(4):
                start = pl.multiple_of((i * 4 + u) * shard, 16)
                block += jnp.dot(
                    turned[i * 4 + u], w_q[h, pl.ds(start, shard), :],
                    preferred_element_type=jnp.float32)
            total[:, cols] = block

        for g in range(2 * h, 2 * h + 2):
            cols = slice(g * 128, (g + 1) * 128)
            mixed[at.z, :, cols] = head(total[:, cols], gain_q[...])

    def project_part(h, which):
        cols = slice(h * 256, (h + 1) * 256)

        @pl.loop(0, 4)
        def _(chip):
            @pl.when(which(chip))
            def _():
                block = total[:, cols]
                for core in range(2):
                    start = pl.multiple_of((chip * 2 + core) * shard, 16)
                    block += jnp.dot(
                        turned[chip * 2 + core], w_q[h, pl.ds(start, shard), :],
                        preferred_element_type=jnp.float32)
                total[:, cols] = block

    def attend_head(h):
        @pl.loop(0, 2)
        def _(tile):
            first = pl.multiple_of(tile * half, half)
            keys = kv[pl.ds(first, span), h * 256:h * 256 + 128]
            values = kv[pl.ds(first, span), h * 256 + 128:h * 256 + 256]
            for g in range(2):
                cols = slice((2 * h + g) * 128, (2 * h + g + 1) * 128)
                scores = lax.dot_general(
                    mixed[at.z, pl.ds(first, half), cols], keys, (((1,), (1,)), ((), ())),
                    preferred_element_type=jnp.float32)
                scores = scores + mask[tile]
                top = jnp.max(scores, axis=-1, keepdims=True)
                weights = jnp.exp2((scores - top) * (query_scale * LOG2_E))
                inverse = 1.0 / jnp.sum(weights, axis=-1, keepdims=True)
                weights = (weights * inverse).astype(jnp.bfloat16)
                mixed[at.z, pl.ds(first, half), cols] = jnp.dot(
                    weights, values, preferred_element_type=jnp.float32).astype(jnp.bfloat16)

    def relay_inner(h):
        @pl.when(at.z == 1)
        def _():
            line_m.falling(1, h)

        @pl.when(at.z == 2)
        def _():
            line_m.rising(1, h)

    def relay_outer(s, h):
        @pl.when(at.z == (1 if s == 1 else 2))
        def _():
            line_m.rising(s, h)

        @pl.when(at.z == (2 if s == 1 else 1))
        def _():
            line_m.falling(s, h)

    project_q(0)
    project_q(1)

    @pl.when(outer)
    def _():
        plane_o[0].first()

    for h in range(heads):
        if h > 1:
            cols = slice(h * 256, (h + 1) * 256)
            total[:, cols] = jnp.zeros((rows, 256), jnp.float32)
            project_part(h, lambda chip: chip != at.chip_d)

            @pl.when(inner)
            def _():
                relay_inner(h - 1)
                plane_q[h].third()

            project_part(h, lambda chip: chip == at.chip_d)
            for g in range(2 * h, 2 * h + 2):
                cols = slice(g * 128, (g + 1) * 128)
                mixed[at.z, :, cols] = head(total[:, cols], gain_q[...])
        halo.need(h)
        attend_head(h)
        line_m.start(h)

        @pl.when(inner)
        def _():
            if h == 1:
                relay_inner(0)
                plane_q[2].first()
                plane_q[3].start()
                plane_q[2].second()
                plane_q[2].sister()
            if h == 2:
                plane_q[3].first()
                plane_o[0].start()
                plane_o[1].start()
                plane_q[3].second()
                plane_q[3].sister()
            if h == 3:
                plane_o[0].first()
                relay_inner(3)

    def output(tile, p):
        some = pl.ds(tile * wide, wide)

        def step(j, _):
            total_o[some, :] += lax.dot_general(
                o_all[j * 2 + p, some, :], mixed[j, :, p * (nq // 2):(p + 1) * (nq // 2)],
                (((1,), (1,)), ((), ())), preferred_element_type=jnp.float32)
        return step

    last = jnp.where(at.z < 2, 3, 0)

    @pl.when(inner)
    def _():
        relay_outer(1, 0)
        relay_outer(1, 1)
        relay_outer(2, 0)
        plane_o[0].second()
        relay_outer(1, 2)
        relay_outer(2, 1)
        relay_outer(1, 3)
        relay_outer(2, 2)
        plane_o[1].first()
        relay_outer(2, 3)

    @pl.when(outer)
    def _():
        plane_o[0].second()
        for s in (1, 2):
            for h in range(heads):
                line_m.step(s, h)
        plane_o[1].first()

    plane_o[0].sister()

    def store(tile):
        some = pl.ds(tile * wide, wide)
        result[some, :] = total_o[some, :].astype(jnp.bfloat16)
        one = pltpu.make_async_copy(result.at[some], out.at[some], local.at[8 + tile])
        one.start()
        return one

    early = lambda j: (j != at.chip_d) & (inner | (j != last))
    far = lambda j: outer & (j == last) & (j != at.chip_d)
    each(early, (0,), output(0, 0), output(0, 1))
    plane_o[1].second()
    plane_o[1].sister()
    each(early, (0,), output(1, 0), output(1, 1))
    line_m.step(3, 0)
    line_m.step(3, 1)
    each(far, (0,), output(0, 0), output(1, 0))
    plane_o[0].third()
    each(lambda j: (j == at.chip_d) & (inner | (j != last)), (0,), output(0, 0), output(0, 1))
    line_m.step(3, 2)
    line_m.step(3, 3)
    each(far, (0,), output(0, 1), output(1, 1))
    each(lambda j: outer & (j == last) & (j == at.chip_d), (0,), output(0, 0), output(0, 1))
    stores = [store(0)]
    plane_o[1].third()
    each(lambda j: j == at.chip_d, (0,), output(1, 0), output(1, 1))
    stores.append(store(1))
    line.finish()
    line_m.finish()
    for plane in [plane_k] + plane_q + plane_o:
        plane.finish()
    halo.finish()
    for one in stores:
        one.wait()


def fused(tokens, w_query, key_weight, value_weight, w_output, query_gain, key_gain):
    rows, depth = tokens.shape
    nq, nk = w_query.shape[1], key_weight.shape[1]
    features = w_output.shape[1]
    freqs = 10000.0 ** (-(jnp.arange(64, dtype=jnp.float32) * 2.0 / HEAD_SIZE))
    freqs = freqs.reshape(1, HEAD_SIZE // 2)
    hbm = pl.BlockSpec(memory_space=pl.ANY)
    bf16, dma = jnp.bfloat16, pltpu.SemaphoreType.DMA
    return pl.pallas_call(
        kernel,
        out_shape=jax.ShapeDtypeStruct((features, rows), bf16),
        in_specs=[hbm] * 8,
        out_specs=hbm,
        scratch_shapes=[
            pltpu.VMEM((4, depth, rows), bf16),
            pltpu.VMEM((8, rows, depth // 2), bf16),
            pltpu.VMEM((4 * depth, 2 * nk), bf16),
            pltpu.VMEM((nq // 256, 4 * depth, 256), bf16),
            pltpu.VMEM((rows, 2 * nk), jnp.float32),
            pltpu.VMEM((8, features, nq // 2), bf16),
            pltpu.VMEM((4, rows, nq), bf16),
            pltpu.VMEM((3 * rows, 2 * nk), bf16),
            pltpu.VMEM((features, rows), jnp.float32),
            pltpu.VMEM((2, rows // 2, rows // 2 + WINDOW_KEYS), jnp.float32),
            pltpu.VMEM((features, rows), bf16),
            pltpu.VMEM((rows, HEAD_SIZE), jnp.float32),
            pltpu.VMEM((rows, HEAD_SIZE), jnp.float32),
            pltpu.VMEM((1, HEAD_SIZE), jnp.float32),
            pltpu.VMEM((1, HEAD_SIZE), jnp.float32),
            pltpu.VMEM((1, HEAD_SIZE // 2), jnp.float32),
            dma((2,)), dma((4, 2)), dma((1,)), dma((7,)), dma((4, 1)), dma((4, 7)),
            dma((2,)), dma((4, 4)), dma((2, 1)), dma((2, 7)), dma((2,)), dma((2, 4)), dma((10,)),
        ],
        compiler_params=pltpu.CompilerParams(
            collective_id=0, has_side_effects=True, vmem_limit_bytes=62 * MIB),
    )(tokens.T, w_query, key_weight, value_weight, w_output.T,
      query_gain.reshape(1, HEAD_SIZE), key_gain.reshape(1, HEAD_SIZE), freqs).T


def solution(mesh):
    small = dict(mesh.shape) == {"seq": 2, "row": 4, "col": 4}
    split = P(("seq", "row"), "col")
    return jax.shard_map(
        fused if small else shards,
        mesh=mesh,
        in_specs=(split, split, split, split, split, P(), P()),
        out_specs=split,
        check_vma=False,
    )
```

```python
import jax
import jax.numpy as jnp
from jax import lax
from jax.experimental import pallas as pl
from jax.experimental.pallas import tpu as pltpu
from jax.sharding import PartitionSpec as P

HEAD_SIZE = 128
WINDOW_KEYS = 1024


query_scale = 168.0 ** (-0.5)


def shifted(block, axis, distance):
    devices = range(lax.axis_size(axis))
    route = [(i - distance, i) for i in devices if i - distance in devices]
    return lax.ppermute(block, axis, route)


def head_norm(block, gain):
    mean_square = jnp.mean(block * block, axis=-1, keepdims=True)
    return block * lax.rsqrt(mean_square + 1e-06) * gain


def rotate(block, positions):
    half = block.shape[-1] // 2
    freqs = 10000.0 ** (-(jnp.arange(half, dtype=jnp.float32) * 2.0 / block.shape[-1]))
    angles = positions.astype(jnp.float32)[:, None] * freqs[None, :]
    cosine = jnp.cos(angles)[:, None, :]
    sine = jnp.sin(angles)[:, None, :]
    first = block[..., :half]
    second = block[..., half:]
    return jnp.concatenate(
        [first * cosine - second * sine, second * cosine + first * sine], axis=-1
    )


def attend(queries, key_states, value_states, qpos, kpos):
    rows = queries.shape[0]
    kv_heads = key_states.shape[1]
    grouped = queries.reshape(rows, kv_heads, 2, HEAD_SIZE)
    scores = (
        jnp.einsum("bhgd,khd->hgbk", grouped, key_states, preferred_element_type=jnp.float32)
        * query_scale
    )
    gap = qpos[:, None] - kpos[None, :]
    valid = (kpos[None, :] >= 0) & (gap >= 0) & (gap < WINDOW_KEYS)
    scores = jnp.where(valid[None, None], scores, -1e30)
    top = jnp.max(scores, axis=-1, keepdims=True)
    weights = jnp.exp(scores - top)
    weights = (weights / jnp.sum(weights, axis=-1, keepdims=True)).astype(jnp.bfloat16)
    mixed = jnp.einsum("hgbk,khd->bhgd", weights, value_states, preferred_element_type=jnp.float32)
    return mixed.astype(jnp.bfloat16).reshape(rows, kv_heads * 2 * HEAD_SIZE)


def shards(tokens, w_query, key_weight, value_weight, w_output, query_gain, key_gain):
    rows = tokens.shape[0]
    whole = lax.all_gather(tokens, "col", axis=1, tiled=True)
    columns = whole
    proj_q = jnp.dot(
        columns,
        lax.all_gather(w_query, ("seq", "row"), axis=0, tiled=True),
        preferred_element_type=jnp.float32,
    )
    projected_key = jnp.dot(
        columns,
        lax.all_gather(key_weight, ("seq", "row"), axis=0, tiled=True),
        preferred_element_type=jnp.float32,
    )
    proj_v = jnp.dot(
        columns,
        lax.all_gather(value_weight, ("seq", "row"), axis=0, tiled=True),
        preferred_element_type=jnp.float32,
    )
    base = lax.axis_index(("seq", "row")) * rows
    positions = base + jnp.arange(rows, dtype=jnp.int32)
    q_heads = proj_q.shape[1] // HEAD_SIZE
    kv_heads = projected_key.shape[1] // HEAD_SIZE
    queries = rotate(
        head_norm(proj_q.reshape(rows, q_heads, HEAD_SIZE), query_gain), positions
    ).astype(jnp.bfloat16)
    key_states = rotate(
        head_norm(projected_key.reshape(rows, kv_heads, HEAD_SIZE), key_gain), positions
    ).astype(jnp.bfloat16)
    key_flat = key_states.reshape(rows, kv_heads * HEAD_SIZE)
    value_flat = proj_v.astype(jnp.bfloat16)
    prior_one = shifted((key_flat, value_flat), ("seq", "row"), 1)
    prior_two = shifted((key_flat, value_flat), ("seq", "row"), 2)
    key_rows = jnp.concatenate([prior_two[0], prior_one[0], key_flat], axis=0).reshape(
        3 * rows, kv_heads, HEAD_SIZE
    )
    value_rows = jnp.concatenate([prior_two[1], prior_one[1], value_flat], axis=0).reshape(
        3 * rows, kv_heads, HEAD_SIZE
    )
    kpos = base - 2 * rows + jnp.arange(3 * rows, dtype=jnp.int32)
    mixed = attend(queries, key_rows, value_rows, positions, kpos)
    all_heads = lax.all_gather(mixed, "col", axis=1, tiled=True)
    columns = all_heads
    attended = jnp.dot(
        columns,
        lax.all_gather(w_output, ("seq", "row"), axis=0, tiled=True),
        preferred_element_type=jnp.float32,
    )
    return attended.astype(jnp.bfloat16)


MESH = pl.DeviceIdType.MESH
MIB = 1 << 20
LOG2_E = 1.4426950408889634


class Place:
    def __init__(self):
        self.y = lax.axis_index("seq")
        row = lax.axis_index("row")
        self.x, self.c = row // 2, row % 2
        self.z = lax.axis_index("col")
        self.to_x = {"seq": self.y, "row": (1 - self.x) * 2 + self.c, "col": self.z}
        self.to_y = {"seq": 1 - self.y, "row": row, "col": self.z}
        self.to_c = {"seq": self.y, "row": self.x * 2 + 1 - self.c, "col": self.z}
        self.up = {"seq": self.y, "row": row, "col": self.z + 1}
        self.down = {"seq": self.y, "row": row, "col": self.z - 1}
        self.to_d = {"seq": 1 - self.y, "row": (1 - self.x) * 2 + self.c, "col": self.z}
        self.chip = self.y * 2 + self.x
        after = (self.chip + 1) % 4
        self.after = {"seq": after // 2, "row": (after % 2) * 2 + self.c, "col": self.z}
        self.chip_x = self.y * 2 + 1 - self.x
        self.chip_y = (1 - self.y) * 2 + self.x
        self.chip_d = (1 - self.y) * 2 + 1 - self.x


def barrier(at):
    sem = pltpu.get_barrier_semaphore()
    for device in (at.to_x, at.to_y, at.to_c, at.to_d):
        pl.semaphore_signal(sem, inc=1, device_id=device, device_id_type=MESH)

    @pl.when(at.z < 3)
    def _():
        pl.semaphore_signal(sem, inc=1, device_id=at.up, device_id_type=MESH)

    @pl.when(at.z > 0)
    def _():
        pl.semaphore_signal(sem, inc=1, device_id=at.down, device_id_type=MESH)

    peers = 4 + (at.z < 3).astype(jnp.int32) + (at.z > 0).astype(jnp.int32)
    pl.semaphore_wait(sem, peers)


class Line:
    def __init__(self, at, whole, part, send, recv):
        self.at, self.whole, self.part, self.send, self.recv = at, whole, part, send, recv

    def copy(self, block, part, way):
        piece = self.part(block, part)
        return pltpu.make_async_remote_copy(
            src_ref=piece, dst_ref=piece,
            send_sem=self.send.at[way], recv_sem=self.recv.at[block, part],
            device_id=self.at.up if way == 0 else self.at.down, device_id_type=MESH)

    def start(self, part):
        at = self.at

        @pl.when(at.z < 3)
        def _():
            self.copy(at.z, part, 0).start()

        @pl.when(at.z > 0)
        def _():
            self.copy(at.z, part, 1).start()

    def rising(self, s, part):
        at = self.at

        @pl.when(at.z - s >= 0)
        def _():
            self.copy(at.z - s, part, 0).wait_recv()

            @pl.when(at.z < 3)
            def _():
                self.copy(at.z - s, part, 0).start()

    def falling(self, s, part):
        at = self.at

        @pl.when(at.z + s <= 3)
        def _():
            self.copy(at.z + s, part, 1).wait_recv()

            @pl.when(at.z > 0)
            def _():
                self.copy(at.z + s, part, 1).start()

    def step(self, s, part):
        self.rising(s, part)
        self.falling(s, part)

    def sent(self, way, blocks):
        piece = self.whole.at[pl.ds(0, blocks)]
        pltpu.make_async_remote_copy(
            src_ref=piece, dst_ref=piece,
            send_sem=self.send.at[way], recv_sem=self.recv.at[0, 0],
            device_id=self.at.up if way == 0 else self.at.down, device_id_type=MESH).wait_send()

    def finish(self):
        for z in range(4):
            @pl.when(self.at.z == z)
            def _():
                if z < 3:
                    self.sent(0, z + 1)
                if z > 0:
                    self.sent(1, 4 - z)


class Plane:
    def __init__(self, at, shards, cut, send, recv):
        self.at, self.shards, self.cut, self.send, self.recv = at, shards, cut, send, recv

    def copy(self, piece, device, slot):
        return pltpu.make_async_remote_copy(
            src_ref=piece, dst_ref=piece, send_sem=self.send.at[0],
            recv_sem=self.recv.at[slot], device_id=device, device_id_type=MESH)

    def half(self, chip, h):
        return self.cut(chip * 2 + self.at.c, h)

    def push(self, chip, h, device, slot):
        self.copy(self.half(chip, h), device, slot).start()

    def share(self, chip):
        self.copy(self.shards(chip * 2 + self.at.c, 1), self.at.to_c, 4).start()

    def need(self, piece, slot):
        self.copy(piece, self.at.to_c, slot).wait_recv()

    def begin(self):
        at = self.at
        self.push(at.chip, 0, at.to_x, 0)
        self.push(at.chip, 1, at.to_y, 1)
        self.share(at.chip)

    def rest(self):
        at = self.at
        self.push(at.chip, 1, at.to_x, 2)
        self.push(at.chip, 0, at.to_y, 2)

    def start(self):
        self.begin()
        self.rest()

    def first(self):
        at = self.at
        self.need(self.half(at.chip_x, 0), 0)
        self.push(at.chip_x, 0, at.to_y, 3)
        self.push(at.chip_x, 0, at.to_c, 4)
        self.need(self.half(at.chip_y, 1), 1)
        self.push(at.chip_y, 1, at.to_x, 6)
        self.push(at.chip_y, 1, at.to_c, 4)

    def second(self):
        at = self.at
        self.need(self.shards(0, 1), 2)
        self.push(at.chip_x, 1, at.to_c, 4)
        self.push(at.chip_y, 0, at.to_c, 4)

    def third(self):
        at = self.at
        self.need(self.half(at.chip_d, 0), 3)
        self.push(at.chip_d, 0, at.to_c, 5)
        self.need(self.half(at.chip_d, 1), 6)
        self.push(at.chip_d, 1, at.to_c, 5)
        self.need(self.shards(0, 1), 5)

    def sister(self):
        self.need(self.shards(0, 3), 4)

    def last(self):
        self.third()
        self.sister()

    def finish(self):
        self.copy(self.shards(0, 7), self.at.to_c, 0).wait_send()


class Halo:
    def __init__(self, at, kv, rows, send, recv):
        self.at, self.kv, self.rows, self.send, self.recv = at, kv, rows, send, recv

    def piece(self, block, h):
        cols = pl.ds(pl.multiple_of(h * 256, 256), 256)
        return self.kv.at[pl.ds(block * self.rows, self.rows), cols]

    def on(self, h):
        return pltpu.make_async_remote_copy(
            src_ref=self.piece(2, h), dst_ref=self.piece(0, h),
            send_sem=self.send.at[0], recv_sem=self.recv.at[0, h],
            device_id=self.at.after, device_id_type=MESH)

    def across(self, block, h):
        return pltpu.make_async_remote_copy(
            src_ref=self.piece(block, h), dst_ref=self.piece(1, h),
            send_sem=self.send.at[1], recv_sem=self.recv.at[1, h],
            device_id=self.at.to_c, device_id_type=MESH)

    def start(self, h):
        @pl.when(self.at.chip < 3)
        def _():
            self.on(h).start()

        @pl.when(self.at.c == 0)
        def _():
            self.across(2, h).start()

    def need(self, h):
        at = self.at

        @pl.when(at.chip > 0)
        def _():
            self.on(h).wait_recv()

            @pl.when(at.c == 1)
            def _():
                self.across(0, h).start()

        @pl.when((at.chip > 0) | (at.c == 1))
        def _():
            self.across(0, h).wait_recv()

    def sent(self, way):
        block = self.kv.at[pl.ds(0, self.rows)]
        pltpu.make_async_remote_copy(
            src_ref=block, dst_ref=block, send_sem=self.send.at[way],
            recv_sem=self.recv.at[0, 0], device_id=self.at.to_c, device_id_type=MESH).wait_send()

    def finish(self):
        at = self.at

        @pl.when(at.chip < 3)
        def _():
            self.sent(0)

        @pl.when((at.chip > 0) | (at.c == 0))
        def _():
            self.sent(1)


def kernel(x, wq, wk, wv, wo, query_gain, key_gain, freqs, out,
           x_all, turned, w_kv, w_q, total, o_all, mixed, kv, total_o, mask, result,
           cosine, sine, gain_q, gain_k, steps,
           zs, zr, ks, kr, qs, qr, ms, mr, os, orr, hs, hr, local):
    at = Place()
    depth, rows = x.shape
    nq, nk = wq.shape[1], wk.shape[1]
    features = wo.shape[0]
    heads = nk // 128
    shard = depth // 2
    device = at.chip * 2 + at.c
    outer = (at.z == 0) | (at.z == 3)
    inner = jnp.logical_not(outer)
    mine = pl.ds(pl.multiple_of(device * shard, 16), shard)
    load_x = pltpu.make_async_copy(x, x_all.at[at.z], local.at[0])
    load_kv = [
        pltpu.make_async_copy(wk, w_kv.at[mine, pl.ds(0, nk)], local.at[1]),
        pltpu.make_async_copy(wv, w_kv.at[mine, pl.ds(nk, nk)], local.at[2]),
    ]
    load_q = [
        pltpu.make_async_copy(wq.at[:, pl.ds(h * 256, 256)], w_q.at[h, mine], local.at[3])
        for h in range(heads)
    ]
    loads_q = pltpu.make_async_copy(w_q.at[:, mine], w_q.at[:, mine], local.at[3])
    load_o = pltpu.make_async_copy(wo, o_all.at[device], local.at[4])
    load_small = [
        pltpu.make_async_copy(query_gain, gain_q, local.at[5]),
        pltpu.make_async_copy(key_gain, gain_k, local.at[6]),
        pltpu.make_async_copy(freqs, steps, local.at[7]),
    ]
    for load in [load_x] + load_kv + load_q + load_small:
        load.start()
    barrier(at)
    half = rows // 2
    wide = features // 2

    def kv_cut(index, h):
        start = pl.multiple_of(index * shard + h * (shard // 2), 16)
        return w_kv.at[pl.ds(start, shard // 2)]

    def kv_shards(index, n):
        return w_kv.at[pl.ds(pl.multiple_of(index * shard, 16), n * shard)]

    def q_cut(head):
        def piece(index, h):
            start = pl.multiple_of(index * shard + h * (shard // 2), 16)
            return w_q.at[head, pl.ds(start, shard // 2)]
        return piece

    def q_shards(head):
        def piece(index, n):
            return w_q.at[head, pl.ds(pl.multiple_of(index * shard, 16), n * shard)]
        return piece

    def o_cut(tile):
        def piece(index, h):
            return o_all.at[index, pl.ds(tile * wide + h * (wide // 2), wide // 2)]
        return piece

    def o_shards(tile):
        def piece(index, n):
            return o_all.at[pl.ds(index, n), pl.ds(tile * wide, wide)]
        return piece

    line = Line(at, x_all, lambda b, p: x_all.at[b, pl.ds(p * shard, shard)], zs, zr)
    line_m = Line(at, mixed, lambda b, p: mixed.at[b, :, pl.ds(p * 256, 256)], ms, mr)
    plane_k = Plane(at, kv_shards, kv_cut, ks, kr)
    plane_q = [Plane(at, q_shards(h), q_cut(h), qs.at[h], qr.at[h]) for h in range(heads)]
    plane_o = [Plane(at, o_shards(t), o_cut(t), os.at[t], orr.at[t]) for t in range(2)]
    halo = Halo(at, kv, rows, hs, hr)

    def apart(distance):
        return lambda j: (j - at.z == distance) | (at.z - j == distance)

    def project(j, p):
        start = pl.multiple_of((j * 2 + p) * shard, 16)
        total[...] += jnp.dot(
            turned[j * 2 + p], w_kv[pl.ds(start, shard), :], preferred_element_type=jnp.float32)

    def each(which, parts, *steps):
        @pl.loop(0, 4)
        def _(j):
            @pl.when(which(j))
            def _():
                for p in parts:
                    for step in steps:
                        step(j, p)

    def turn(j, p):
        turned[j * 2 + p] = x_all[j, p * shard:(p + 1) * shard, :].T

    load_x.wait()
    line.start(0)
    for load in load_kv:
        load.wait()
    plane_k.start()
    line.start(1)
    load_o.start()
    turn(at.z, 0)
    turn(at.z, 1)
    total[...] = jnp.zeros_like(total)
    total_o[...] = jnp.zeros_like(total_o)

    @pl.when(at.chip == 0)
    def _():
        kv[pl.ds(0, rows), :] = jnp.zeros((rows, 2 * nk), jnp.bfloat16)

        @pl.when(at.c == 0)
        def _():
            kv[pl.ds(rows, rows), :] = jnp.zeros((rows, 2 * nk), jnp.bfloat16)

    loads_q.wait()
    load_o.wait()
    for load in load_small:
        load.wait()

    plane_k.first()
    plane_q[0].start()
    plane_q[1].start()
    line.step(1, 0)

    positions = device * rows + lax.broadcasted_iota(jnp.int32, (rows, 128), 0)
    angles = positions.astype(jnp.float32) * jnp.concatenate([steps[...], steps[...]], axis=1)
    lower = lax.broadcasted_iota(jnp.int32, (rows, 128), 1) < 64
    cosine[...] = jnp.cos(angles)
    turned_sine = jnp.sin(angles)
    sine[...] = jnp.where(lower, -turned_sine, turned_sine)

    span = half + 2 * rows
    for tile in range(2):
        query = lax.broadcasted_iota(jnp.int32, (half, span), 0)
        key = lax.broadcasted_iota(jnp.int32, (half, span), 1)
        low = 2 * rows - device * rows - tile * half
        valid = (key > query) & (key <= query + WINDOW_KEYS) & (key >= low)
        mask[tile] = jnp.where(valid, 0.0, -1e30)

    each(apart(1), (0,), turn)
    plane_k.second()
    line.step(1, 1)
    each(apart(1), (1,), turn)
    line.step(2, 0)
    plane_k.last()
    each(apart(0), (0, 1), project)
    each(apart(1), (0, 1), project)
    plane_q[0].first()
    plane_q[0].second()
    each(apart(2), (0,), turn, project)
    line.step(2, 1)
    plane_q[1].first()

    @pl.when(outer)
    def _():
        plane_q[2].start()
        plane_q[3].start()

    each(apart(2), (1,), turn, project)
    plane_q[0].last()
    plane_q[1].second()

    @pl.when(outer)
    def _():
        plane_q[1].last()
        line.step(3, 0)

    each(apart(3), (0,), turn, project)

    @pl.when(outer)
    def _():
        plane_q[2].first()
        plane_q[2].second()
        plane_q[3].first()
        plane_o[0].begin()
        plane_q[3].second()
        plane_q[2].last()
        line.step(3, 1)

    each(apart(3), (1,), turn, project)

    def head(block, gain):
        mean_square = jnp.mean(block * block, axis=-1, keepdims=True)
        normed = block * lax.rsqrt(mean_square + 1e-06) * gain
        spun = normed * cosine[...] + pltpu.roll(normed, 64, 1) * sine[...]
        return spun.astype(jnp.bfloat16)

    own = pl.ds(2 * rows, rows)

    @pl.loop(0, heads)
    def _(h):
        keys = total[:, pl.ds(pl.multiple_of(h * 128, 128), 128)]
        kv[own, pl.ds(pl.multiple_of(h * 256, 256), 128)] = head(keys, gain_k[...])
        values = total[:, pl.ds(pl.multiple_of(nk + h * 128, 128), 128)]
        kv[own, pl.ds(pl.multiple_of(h * 256 + 128, 128), 128)] = values.astype(jnp.bfloat16)
        halo.start(h)

        @pl.when(inner & (h == 1))
        def _():
            plane_q[2].start()

    @pl.when(inner)
    def _():
        plane_q[1].last()

    @pl.when(outer)
    def _():
        plane_o[0].rest()
        plane_o[1].start()
        plane_q[3].last()

    def project_q(h):
        cols = slice(h * 256, (h + 1) * 256)
        total[:, cols] = jnp.zeros((rows, 256), jnp.float32)

        @pl.loop(0, 2)
        def _(i):
            block = total[:, cols]
            for u in range(4):
                start = pl.multiple_of((i * 4 + u) * shard, 16)
                block += jnp.dot(
                    turned[i * 4 + u], w_q[h, pl.ds(start, shard), :],
                    preferred_element_type=jnp.float32)
            total[:, cols] = block

        for g in range(2 * h, 2 * h + 2):
            cols = slice(g * 128, (g + 1) * 128)
            mixed[at.z, :, cols] = head(total[:, cols], gain_q[...])

    def project_part(h, which):
        cols = slice(h * 256, (h + 1) * 256)

        @pl.loop(0, 4)
        def _(chip):
            @pl.when(which(chip))
            def _():
                block = total[:, cols]
                for core in range(2):
                    start = pl.multiple_of((chip * 2 + core) * shard, 16)
                    block += jnp.dot(
                        turned[chip * 2 + core], w_q[h, pl.ds(start, shard), :],
                        preferred_element_type=jnp.float32)
                total[:, cols] = block

    def attend_head(h):
        @pl.loop(0, 2)
        def _(tile):
            first = pl.multiple_of(tile * half, half)
            keys = kv[pl.ds(first, span), h * 256:h * 256 + 128]
            values = kv[pl.ds(first, span), h * 256 + 128:h * 256 + 256]
            for g in range(2):
                cols = slice((2 * h + g) * 128, (2 * h + g + 1) * 128)
                scores = lax.dot_general(
                    mixed[at.z, pl.ds(first, half), cols], keys, (((1,), (1,)), ((), ())),
                    preferred_element_type=jnp.float32)
                scores = scores + mask[tile]
                top = jnp.max(scores, axis=-1, keepdims=True)
                weights = jnp.exp2((scores - top) * (query_scale * LOG2_E))
                inverse = 1.0 / jnp.sum(weights, axis=-1, keepdims=True)
                weights = (weights * inverse).astype(jnp.bfloat16)
                mixed[at.z, pl.ds(first, half), cols] = jnp.dot(
                    weights, values, preferred_element_type=jnp.float32).astype(jnp.bfloat16)

    def relay_inner(h):
        @pl.when(at.z == 1)
        def _():
            line_m.falling(1, h)

        @pl.when(at.z == 2)
        def _():
            line_m.rising(1, h)

    def relay_outer(s, h):
        @pl.when(at.z == (1 if s == 1 else 2))
        def _():
            line_m.rising(s, h)

        @pl.when(at.z == (2 if s == 1 else 1))
        def _():
            line_m.falling(s, h)

    project_q(0)
    project_q(1)

    @pl.when(outer)
    def _():
        plane_o[0].first()

    for h in range(heads):
        if h > 1:
            cols = slice(h * 256, (h + 1) * 256)
            total[:, cols] = jnp.zeros((rows, 256), jnp.float32)
            project_part(h, lambda chip: chip != at.chip_d)

            @pl.when(inner)
            def _():
                plane_q[h].third()

            project_part(h, lambda chip: chip == at.chip_d)
            for g in range(2 * h, 2 * h + 2):
                cols = slice(g * 128, (g + 1) * 128)
                mixed[at.z, :, cols] = head(total[:, cols], gain_q[...])
        if h > 1:
            @pl.when(inner)
            def _():
                relay_inner(h - 1)

        halo.need(h)
        attend_head(h)
        line_m.start(h)

        @pl.when(inner)
        def _():
            if h == 1:
                relay_inner(0)
                plane_q[2].first()
                plane_q[3].start()
                plane_q[2].second()
                plane_q[2].sister()
            if h == 2:
                plane_q[3].first()
                plane_o[0].start()
                plane_o[1].start()
                plane_q[3].second()
                plane_q[3].sister()
            if h == 3:
                plane_o[0].first()
                relay_inner(3)

    def output(tile, p):
        some = pl.ds(tile * wide, wide)

        def step(j, _):
            total_o[some, :] += lax.dot_general(
                o_all[j * 2 + p, some, :], mixed[j, :, p * (nq // 2):(p + 1) * (nq // 2)],
                (((1,), (1,)), ((), ())), preferred_element_type=jnp.float32)
        return step

    last = jnp.where(at.z < 2, 3, 0)

    @pl.when(inner)
    def _():
        relay_outer(1, 0)
        relay_outer(1, 1)
        relay_outer(2, 0)
        plane_o[0].second()
        relay_outer(1, 2)
        relay_outer(2, 1)
        relay_outer(1, 3)
        relay_outer(2, 2)
        plane_o[1].first()
        relay_outer(2, 3)

    @pl.when(outer)
    def _():
        plane_o[0].second()
        for s in (1, 2):
            for h in range(heads):
                line_m.step(s, h)
        plane_o[1].first()

    plane_o[0].sister()

    def store(tile):
        some = pl.ds(tile * wide, wide)
        result[some, :] = total_o[some, :].astype(jnp.bfloat16)
        one = pltpu.make_async_copy(result.at[some], out.at[some], local.at[8 + tile])
        one.start()
        return one

    early = lambda j: (j != at.chip_d) & (inner | (j != last))
    far = lambda j: outer & (j == last) & (j != at.chip_d)
    each(early, (0,), output(0, 0), output(0, 1))
    plane_o[1].second()
    plane_o[1].sister()
    each(early, (0,), output(1, 0), output(1, 1))
    line_m.step(3, 0)
    line_m.step(3, 1)
    each(far, (0,), output(0, 0), output(1, 0))
    plane_o[0].third()
    each(lambda j: (j == at.chip_d) & (inner | (j != last)), (0,), output(0, 0), output(0, 1))
    line_m.step(3, 2)
    line_m.step(3, 3)
    each(far, (0,), output(0, 1), output(1, 1))
    each(lambda j: outer & (j == last) & (j == at.chip_d), (0,), output(0, 0), output(0, 1))
    stores = [store(0)]
    plane_o[1].third()
    each(lambda j: j == at.chip_d, (0,), output(1, 0), output(1, 1))
    stores.append(store(1))
    line.finish()
    line_m.finish()
    for plane in [plane_k] + plane_q + plane_o:
        plane.finish()
    halo.finish()
    for one in stores:
        one.wait()


def fused(tokens, w_query, key_weight, value_weight, w_output, query_gain, key_gain):
    rows, depth = tokens.shape
    nq, nk = w_query.shape[1], key_weight.shape[1]
    features = w_output.shape[1]
    freqs = 10000.0 ** (-(jnp.arange(64, dtype=jnp.float32) * 2.0 / HEAD_SIZE))
    freqs = freqs.reshape(1, HEAD_SIZE // 2)
    hbm = pl.BlockSpec(memory_space=pl.ANY)
    bf16, dma = jnp.bfloat16, pltpu.SemaphoreType.DMA
    return pl.pallas_call(
        kernel,
        out_shape=jax.ShapeDtypeStruct((features, rows), bf16),
        in_specs=[hbm] * 8,
        out_specs=hbm,
        scratch_shapes=[
            pltpu.VMEM((4, depth, rows), bf16),
            pltpu.VMEM((8, rows, depth // 2), bf16),
            pltpu.VMEM((4 * depth, 2 * nk), bf16),
            pltpu.VMEM((nq // 256, 4 * depth, 256), bf16),
            pltpu.VMEM((rows, 2 * nk), jnp.float32),
            pltpu.VMEM((8, features, nq // 2), bf16),
            pltpu.VMEM((4, rows, nq), bf16),
            pltpu.VMEM((3 * rows, 2 * nk), bf16),
            pltpu.VMEM((features, rows), jnp.float32),
            pltpu.VMEM((2, rows // 2, rows // 2 + WINDOW_KEYS), jnp.float32),
            pltpu.VMEM((features, rows), bf16),
            pltpu.VMEM((rows, HEAD_SIZE), jnp.float32),
            pltpu.VMEM((rows, HEAD_SIZE), jnp.float32),
            pltpu.VMEM((1, HEAD_SIZE), jnp.float32),
            pltpu.VMEM((1, HEAD_SIZE), jnp.float32),
            pltpu.VMEM((1, HEAD_SIZE // 2), jnp.float32),
            dma((2,)), dma((4, 2)), dma((1,)), dma((7,)), dma((4, 1)), dma((4, 7)),
            dma((2,)), dma((4, 4)), dma((2, 1)), dma((2, 7)), dma((2,)), dma((2, 4)), dma((10,)),
        ],
        compiler_params=pltpu.CompilerParams(
            collective_id=0, has_side_effects=True, vmem_limit_bytes=62 * MIB),
    )(tokens.T, w_query, key_weight, value_weight, w_output.T,
      query_gain.reshape(1, HEAD_SIZE), key_gain.reshape(1, HEAD_SIZE), freqs).T


def solution(mesh):
    small = dict(mesh.shape) == {"seq": 2, "row": 4, "col": 4}
    split = P(("seq", "row"), "col")
    return jax.shard_map(
        fused if small else shards,
        mesh=mesh,
        in_specs=(split, split, split, split, split, P(), P()),
        out_specs=split,
        check_vma=False,
    )
```

```python
import jax
import jax.numpy as jnp
from jax import lax
from jax.experimental import pallas as pl
from jax.experimental.pallas import tpu as pltpu
from jax.sharding import PartitionSpec as P

HEAD_SIZE = 128
WINDOW_KEYS = 1024


query_scale = 168.0 ** (-0.5)


def shifted(block, axis, distance):
    devices = range(lax.axis_size(axis))
    route = [(i - distance, i) for i in devices if i - distance in devices]
    return lax.ppermute(block, axis, route)


def head_norm(block, gain):
    mean_square = jnp.mean(block * block, axis=-1, keepdims=True)
    return block * lax.rsqrt(mean_square + 1e-06) * gain


def rotate(block, positions):
    half = block.shape[-1] // 2
    freqs = 10000.0 ** (-(jnp.arange(half, dtype=jnp.float32) * 2.0 / block.shape[-1]))
    angles = positions.astype(jnp.float32)[:, None] * freqs[None, :]
    cosine = jnp.cos(angles)[:, None, :]
    sine = jnp.sin(angles)[:, None, :]
    first = block[..., :half]
    second = block[..., half:]
    return jnp.concatenate(
        [first * cosine - second * sine, second * cosine + first * sine], axis=-1
    )


def attend(queries, key_states, value_states, qpos, kpos):
    rows = queries.shape[0]
    kv_heads = key_states.shape[1]
    grouped = queries.reshape(rows, kv_heads, 2, HEAD_SIZE)
    scores = (
        jnp.einsum("bhgd,khd->hgbk", grouped, key_states, preferred_element_type=jnp.float32)
        * query_scale
    )
    gap = qpos[:, None] - kpos[None, :]
    valid = (kpos[None, :] >= 0) & (gap >= 0) & (gap < WINDOW_KEYS)
    scores = jnp.where(valid[None, None], scores, -1e30)
    top = jnp.max(scores, axis=-1, keepdims=True)
    weights = jnp.exp(scores - top)
    weights = (weights / jnp.sum(weights, axis=-1, keepdims=True)).astype(jnp.bfloat16)
    mixed = jnp.einsum("hgbk,khd->bhgd", weights, value_states, preferred_element_type=jnp.float32)
    return mixed.astype(jnp.bfloat16).reshape(rows, kv_heads * 2 * HEAD_SIZE)


def shards(tokens, w_query, key_weight, value_weight, w_output, query_gain, key_gain):
    rows = tokens.shape[0]
    whole = lax.all_gather(tokens, "col", axis=1, tiled=True)
    columns = whole
    proj_q = jnp.dot(
        columns,
        lax.all_gather(w_query, ("seq", "row"), axis=0, tiled=True),
        preferred_element_type=jnp.float32,
    )
    projected_key = jnp.dot(
        columns,
        lax.all_gather(key_weight, ("seq", "row"), axis=0, tiled=True),
        preferred_element_type=jnp.float32,
    )
    proj_v = jnp.dot(
        columns,
        lax.all_gather(value_weight, ("seq", "row"), axis=0, tiled=True),
        preferred_element_type=jnp.float32,
    )
    base = lax.axis_index(("seq", "row")) * rows
    positions = base + jnp.arange(rows, dtype=jnp.int32)
    q_heads = proj_q.shape[1] // HEAD_SIZE
    kv_heads = projected_key.shape[1] // HEAD_SIZE
    queries = rotate(
        head_norm(proj_q.reshape(rows, q_heads, HEAD_SIZE), query_gain), positions
    ).astype(jnp.bfloat16)
    key_states = rotate(
        head_norm(projected_key.reshape(rows, kv_heads, HEAD_SIZE), key_gain), positions
    ).astype(jnp.bfloat16)
    key_flat = key_states.reshape(rows, kv_heads * HEAD_SIZE)
    value_flat = proj_v.astype(jnp.bfloat16)
    prior_one = shifted((key_flat, value_flat), ("seq", "row"), 1)
    prior_two = shifted((key_flat, value_flat), ("seq", "row"), 2)
    key_rows = jnp.concatenate([prior_two[0], prior_one[0], key_flat], axis=0).reshape(
        3 * rows, kv_heads, HEAD_SIZE
    )
    value_rows = jnp.concatenate([prior_two[1], prior_one[1], value_flat], axis=0).reshape(
        3 * rows, kv_heads, HEAD_SIZE
    )
    kpos = base - 2 * rows + jnp.arange(3 * rows, dtype=jnp.int32)
    mixed = attend(queries, key_rows, value_rows, positions, kpos)
    all_heads = lax.all_gather(mixed, "col", axis=1, tiled=True)
    columns = all_heads
    attended = jnp.dot(
        columns,
        lax.all_gather(w_output, ("seq", "row"), axis=0, tiled=True),
        preferred_element_type=jnp.float32,
    )
    return attended.astype(jnp.bfloat16)


MESH = pl.DeviceIdType.MESH
MIB = 1 << 20
LOG2_E = 1.4426950408889634


class Place:
    def __init__(self):
        self.y = lax.axis_index("seq")
        row = lax.axis_index("row")
        self.x, self.c = row // 2, row % 2
        self.z = lax.axis_index("col")
        self.to_x = {"seq": self.y, "row": (1 - self.x) * 2 + self.c, "col": self.z}
        self.to_y = {"seq": 1 - self.y, "row": row, "col": self.z}
        self.to_c = {"seq": self.y, "row": self.x * 2 + 1 - self.c, "col": self.z}
        self.up = {"seq": self.y, "row": row, "col": self.z + 1}
        self.down = {"seq": self.y, "row": row, "col": self.z - 1}
        self.to_d = {"seq": 1 - self.y, "row": (1 - self.x) * 2 + self.c, "col": self.z}
        self.chip = self.y * 2 + self.x
        after = (self.chip + 1) % 4
        self.after = {"seq": after // 2, "row": (after % 2) * 2 + self.c, "col": self.z}
        self.chip_x = self.y * 2 + 1 - self.x
        self.chip_y = (1 - self.y) * 2 + self.x
        self.chip_d = (1 - self.y) * 2 + 1 - self.x


def barrier(at):
    sem = pltpu.get_barrier_semaphore()
    for device in (at.to_x, at.to_y, at.to_c, at.to_d):
        pl.semaphore_signal(sem, inc=1, device_id=device, device_id_type=MESH)

    @pl.when(at.z < 3)
    def _():
        pl.semaphore_signal(sem, inc=1, device_id=at.up, device_id_type=MESH)

    @pl.when(at.z > 0)
    def _():
        pl.semaphore_signal(sem, inc=1, device_id=at.down, device_id_type=MESH)

    peers = 4 + (at.z < 3).astype(jnp.int32) + (at.z > 0).astype(jnp.int32)
    pl.semaphore_wait(sem, peers)


class Line:
    def __init__(self, at, whole, part, send, recv):
        self.at, self.whole, self.part, self.send, self.recv = at, whole, part, send, recv

    def copy(self, block, part, way):
        piece = self.part(block, part)
        return pltpu.make_async_remote_copy(
            src_ref=piece, dst_ref=piece,
            send_sem=self.send.at[way], recv_sem=self.recv.at[block, part],
            device_id=self.at.up if way == 0 else self.at.down, device_id_type=MESH)

    def start(self, part):
        at = self.at

        @pl.when(at.z < 3)
        def _():
            self.copy(at.z, part, 0).start()

        @pl.when(at.z > 0)
        def _():
            self.copy(at.z, part, 1).start()

    def rising(self, s, part):
        at = self.at

        @pl.when(at.z - s >= 0)
        def _():
            self.copy(at.z - s, part, 0).wait_recv()

            @pl.when(at.z < 3)
            def _():
                self.copy(at.z - s, part, 0).start()

    def falling(self, s, part):
        at = self.at

        @pl.when(at.z + s <= 3)
        def _():
            self.copy(at.z + s, part, 1).wait_recv()

            @pl.when(at.z > 0)
            def _():
                self.copy(at.z + s, part, 1).start()

    def step(self, s, part):
        self.rising(s, part)
        self.falling(s, part)

    def sent(self, way, blocks):
        piece = self.whole.at[pl.ds(0, blocks)]
        pltpu.make_async_remote_copy(
            src_ref=piece, dst_ref=piece,
            send_sem=self.send.at[way], recv_sem=self.recv.at[0, 0],
            device_id=self.at.up if way == 0 else self.at.down, device_id_type=MESH).wait_send()

    def finish(self):
        for z in range(4):
            @pl.when(self.at.z == z)
            def _():
                if z < 3:
                    self.sent(0, z + 1)
                if z > 0:
                    self.sent(1, 4 - z)


class Plane:
    def __init__(self, at, shards, cut, send, recv):
        self.at, self.shards, self.cut, self.send, self.recv = at, shards, cut, send, recv

    def copy(self, piece, device, slot):
        return pltpu.make_async_remote_copy(
            src_ref=piece, dst_ref=piece, send_sem=self.send.at[0],
            recv_sem=self.recv.at[slot], device_id=device, device_id_type=MESH)

    def half(self, chip, h):
        return self.cut(chip * 2 + self.at.c, h)

    def push(self, chip, h, device, slot):
        self.copy(self.half(chip, h), device, slot).start()

    def share(self, chip):
        self.copy(self.shards(chip * 2 + self.at.c, 1), self.at.to_c, 4).start()

    def need(self, piece, slot):
        self.copy(piece, self.at.to_c, slot).wait_recv()

    def begin(self):
        at = self.at
        self.push(at.chip, 0, at.to_x, 0)
        self.push(at.chip, 1, at.to_y, 1)
        self.share(at.chip)

    def rest(self):
        at = self.at
        self.push(at.chip, 1, at.to_x, 2)
        self.push(at.chip, 0, at.to_y, 2)

    def start(self):
        self.begin()
        self.rest()

    def first(self):
        at = self.at
        self.need(self.half(at.chip_x, 0), 0)
        self.push(at.chip_x, 0, at.to_y, 3)
        self.push(at.chip_x, 0, at.to_c, 4)
        self.need(self.half(at.chip_y, 1), 1)
        self.push(at.chip_y, 1, at.to_x, 6)
        self.push(at.chip_y, 1, at.to_c, 4)

    def second(self):
        at = self.at
        self.need(self.shards(0, 1), 2)
        self.push(at.chip_x, 1, at.to_c, 4)
        self.push(at.chip_y, 0, at.to_c, 4)

    def third(self):
        at = self.at
        self.need(self.half(at.chip_d, 0), 3)
        self.push(at.chip_d, 0, at.to_c, 5)
        self.need(self.half(at.chip_d, 1), 6)
        self.push(at.chip_d, 1, at.to_c, 5)
        self.need(self.shards(0, 1), 5)

    def sister(self):
        self.need(self.shards(0, 3), 4)

    def last(self):
        self.third()
        self.sister()

    def finish(self):
        self.copy(self.shards(0, 7), self.at.to_c, 0).wait_send()


class Halo:
    def __init__(self, at, kv, rows, send, recv):
        self.at, self.kv, self.rows, self.send, self.recv = at, kv, rows, send, recv

    def piece(self, block, h):
        cols = pl.ds(pl.multiple_of(h * 256, 256), 256)
        return self.kv.at[pl.ds(block * self.rows, self.rows), cols]

    def on(self, h):
        return pltpu.make_async_remote_copy(
            src_ref=self.piece(2, h), dst_ref=self.piece(0, h),
            send_sem=self.send.at[0], recv_sem=self.recv.at[0, h],
            device_id=self.at.after, device_id_type=MESH)

    def across(self, block, h):
        return pltpu.make_async_remote_copy(
            src_ref=self.piece(block, h), dst_ref=self.piece(1, h),
            send_sem=self.send.at[1], recv_sem=self.recv.at[1, h],
            device_id=self.at.to_c, device_id_type=MESH)

    def start(self, h):
        @pl.when(self.at.chip < 3)
        def _():
            self.on(h).start()

        @pl.when(self.at.c == 0)
        def _():
            self.across(2, h).start()

    def need(self, h):
        at = self.at

        @pl.when(at.chip > 0)
        def _():
            self.on(h).wait_recv()

            @pl.when(at.c == 1)
            def _():
                self.across(0, h).start()

        @pl.when((at.chip > 0) | (at.c == 1))
        def _():
            self.across(0, h).wait_recv()

    def sent(self, way):
        block = self.kv.at[pl.ds(0, self.rows)]
        pltpu.make_async_remote_copy(
            src_ref=block, dst_ref=block, send_sem=self.send.at[way],
            recv_sem=self.recv.at[0, 0], device_id=self.at.to_c, device_id_type=MESH).wait_send()

    def finish(self):
        at = self.at

        @pl.when(at.chip < 3)
        def _():
            self.sent(0)

        @pl.when((at.chip > 0) | (at.c == 0))
        def _():
            self.sent(1)


def kernel(x, wq, wk, wv, wo, query_gain, key_gain, freqs, out,
           x_all, turned, w_kv, w_q, total, o_all, mixed, kv, total_o, mask, result,
           cosine, sine, gain_q, gain_k, steps,
           zs, zr, ks, kr, qs, qr, ms, mr, os, orr, hs, hr, local):
    at = Place()
    depth, rows = x.shape
    nq, nk = wq.shape[1], wk.shape[1]
    features = wo.shape[0]
    heads = nk // 128
    shard = depth // 2
    device = at.chip * 2 + at.c
    outer = (at.z == 0) | (at.z == 3)
    inner = jnp.logical_not(outer)
    mine = pl.ds(pl.multiple_of(device * shard, 16), shard)
    load_x = pltpu.make_async_copy(x, x_all.at[at.z], local.at[0])
    load_kv = [
        pltpu.make_async_copy(wk, w_kv.at[mine, pl.ds(0, nk)], local.at[1]),
        pltpu.make_async_copy(wv, w_kv.at[mine, pl.ds(nk, nk)], local.at[2]),
    ]
    load_q = [
        pltpu.make_async_copy(wq.at[:, pl.ds(h * 256, 256)], w_q.at[h, mine], local.at[3])
        for h in range(heads)
    ]
    loads_q = pltpu.make_async_copy(w_q.at[:, mine], w_q.at[:, mine], local.at[3])
    load_o = pltpu.make_async_copy(wo, o_all.at[device], local.at[4])
    load_small = [
        pltpu.make_async_copy(query_gain, gain_q, local.at[5]),
        pltpu.make_async_copy(key_gain, gain_k, local.at[6]),
        pltpu.make_async_copy(freqs, steps, local.at[7]),
    ]
    for load in [load_x] + load_kv + load_q + load_small:
        load.start()
    barrier(at)
    half = rows // 2
    wide = features // 2

    def kv_cut(index, h):
        start = pl.multiple_of(index * shard + h * (shard // 2), 16)
        return w_kv.at[pl.ds(start, shard // 2)]

    def kv_shards(index, n):
        return w_kv.at[pl.ds(pl.multiple_of(index * shard, 16), n * shard)]

    def q_cut(head):
        def piece(index, h):
            start = pl.multiple_of(index * shard + h * (shard // 2), 16)
            return w_q.at[head, pl.ds(start, shard // 2)]
        return piece

    def q_shards(head):
        def piece(index, n):
            return w_q.at[head, pl.ds(pl.multiple_of(index * shard, 16), n * shard)]
        return piece

    def o_cut(tile):
        def piece(index, h):
            return o_all.at[index, pl.ds(tile * wide + h * (wide // 2), wide // 2)]
        return piece

    def o_shards(tile):
        def piece(index, n):
            return o_all.at[pl.ds(index, n), pl.ds(tile * wide, wide)]
        return piece

    line = Line(at, x_all, lambda b, p: x_all.at[b, pl.ds(p * shard, shard)], zs, zr)
    line_m = Line(at, mixed, lambda b, p: mixed.at[b, :, pl.ds(p * 256, 256)], ms, mr)
    plane_k = Plane(at, kv_shards, kv_cut, ks, kr)
    plane_q = [Plane(at, q_shards(h), q_cut(h), qs.at[h], qr.at[h]) for h in range(heads)]
    plane_o = [Plane(at, o_shards(t), o_cut(t), os.at[t], orr.at[t]) for t in range(2)]
    halo = Halo(at, kv, rows, hs, hr)

    def apart(distance):
        return lambda j: (j - at.z == distance) | (at.z - j == distance)

    def project(j, p):
        start = pl.multiple_of((j * 2 + p) * shard, 16)
        total[...] += jnp.dot(
            turned[j * 2 + p], w_kv[pl.ds(start, shard), :], preferred_element_type=jnp.float32)

    def each(which, parts, *steps):
        @pl.loop(0, 4)
        def _(j):
            @pl.when(which(j))
            def _():
                for p in parts:
                    for step in steps:
                        step(j, p)

    def turn(j, p):
        turned[j * 2 + p] = x_all[j, p * shard:(p + 1) * shard, :].T

    load_x.wait()
    line.start(0)
    for load in load_kv:
        load.wait()
    plane_k.start()
    line.start(1)
    load_o.start()
    turn(at.z, 0)
    turn(at.z, 1)
    total[...] = jnp.zeros_like(total)
    total_o[...] = jnp.zeros_like(total_o)

    @pl.when(at.chip == 0)
    def _():
        kv[pl.ds(0, rows), :] = jnp.zeros((rows, 2 * nk), jnp.bfloat16)

        @pl.when(at.c == 0)
        def _():
            kv[pl.ds(rows, rows), :] = jnp.zeros((rows, 2 * nk), jnp.bfloat16)

    loads_q.wait()
    load_o.wait()
    for load in load_small:
        load.wait()

    plane_k.first()
    plane_q[0].start()
    plane_q[1].start()
    line.step(1, 0)

    positions = device * rows + lax.broadcasted_iota(jnp.int32, (rows, 128), 0)
    angles = positions.astype(jnp.float32) * jnp.concatenate([steps[...], steps[...]], axis=1)
    lower = lax.broadcasted_iota(jnp.int32, (rows, 128), 1) < 64
    cosine[...] = jnp.cos(angles)
    turned_sine = jnp.sin(angles)
    sine[...] = jnp.where(lower, -turned_sine, turned_sine)

    span = half + 2 * rows
    for tile in range(2):
        query = lax.broadcasted_iota(jnp.int32, (half, span), 0)
        key = lax.broadcasted_iota(jnp.int32, (half, span), 1)
        low = 2 * rows - device * rows - tile * half
        valid = (key > query) & (key <= query + WINDOW_KEYS) & (key >= low)
        mask[tile] = jnp.where(valid, 0.0, -1e30)

    each(apart(1), (0,), turn)
    plane_k.second()
    line.step(1, 1)
    each(apart(1), (1,), turn)
    line.step(2, 0)
    plane_k.last()
    each(apart(0), (0, 1), project)
    each(apart(1), (0, 1), project)
    plane_q[0].first()
    plane_q[0].second()
    each(apart(2), (0,), turn, project)
    line.step(2, 1)
    plane_q[1].first()

    @pl.when(outer)
    def _():
        plane_q[2].start()
        plane_q[3].start()

    each(apart(2), (1,), turn, project)
    plane_q[0].last()
    plane_q[1].second()

    @pl.when(outer)
    def _():
        plane_q[1].last()
        line.step(3, 0)

    each(apart(3), (0,), turn, project)

    @pl.when(outer)
    def _():
        plane_q[2].first()
        plane_q[2].second()
        plane_q[3].first()
        plane_o[0].begin()
        plane_q[3].second()
        plane_q[2].last()
        line.step(3, 1)

    each(apart(3), (1,), turn, project)

    def head(block, gain):
        mean_square = jnp.mean(block * block, axis=-1, keepdims=True)
        normed = block * lax.rsqrt(mean_square + 1e-06) * gain
        spun = normed * cosine[...] + pltpu.roll(normed, 64, 1) * sine[...]
        return spun.astype(jnp.bfloat16)

    own = pl.ds(2 * rows, rows)

    @pl.loop(0, heads)
    def _(h):
        keys = total[:, pl.ds(pl.multiple_of(h * 128, 128), 128)]
        kv[own, pl.ds(pl.multiple_of(h * 256, 256), 128)] = head(keys, gain_k[...])
        values = total[:, pl.ds(pl.multiple_of(nk + h * 128, 128), 128)]
        kv[own, pl.ds(pl.multiple_of(h * 256 + 128, 128), 128)] = values.astype(jnp.bfloat16)
        halo.start(h)

        @pl.when(inner & (h == 1))
        def _():
            plane_q[2].start()

    @pl.when(inner)
    def _():
        plane_q[1].last()

    @pl.when(outer)
    def _():
        plane_o[0].rest()
        plane_o[1].start()
        plane_q[3].last()

    def project_q(h):
        cols = slice(h * 256, (h + 1) * 256)
        total[:, cols] = jnp.zeros((rows, 256), jnp.float32)

        @pl.loop(0, 2)
        def _(i):
            block = total[:, cols]
            for u in range(4):
                start = pl.multiple_of((i * 4 + u) * shard, 16)
                block += jnp.dot(
                    turned[i * 4 + u], w_q[h, pl.ds(start, shard), :],
                    preferred_element_type=jnp.float32)
            total[:, cols] = block

        for g in range(2 * h, 2 * h + 2):
            cols = slice(g * 128, (g + 1) * 128)
            mixed[at.z, :, cols] = head(total[:, cols], gain_q[...])

    def project_part(h, which):
        cols = slice(h * 256, (h + 1) * 256)

        @pl.loop(0, 4)
        def _(chip):
            @pl.when(which(chip))
            def _():
                block = total[:, cols]
                for core in range(2):
                    start = pl.multiple_of((chip * 2 + core) * shard, 16)
                    block += jnp.dot(
                        turned[chip * 2 + core], w_q[h, pl.ds(start, shard), :],
                        preferred_element_type=jnp.float32)
                total[:, cols] = block

    def attend_head(h):
        @pl.loop(0, 2)
        def _(tile):
            first = pl.multiple_of(tile * half, half)
            keys = kv[pl.ds(first, span), h * 256:h * 256 + 128]
            values = kv[pl.ds(first, span), h * 256 + 128:h * 256 + 256]
            for g in range(2):
                cols = slice((2 * h + g) * 128, (2 * h + g + 1) * 128)
                scores = lax.dot_general(
                    mixed[at.z, pl.ds(first, half), cols], keys, (((1,), (1,)), ((), ())),
                    preferred_element_type=jnp.float32)
                scores = scores + mask[tile]
                top = jnp.max(scores, axis=-1, keepdims=True)
                weights = jnp.exp2((scores - top) * (query_scale * LOG2_E))
                inverse = 1.0 / jnp.sum(weights, axis=-1, keepdims=True)
                weights = (weights * inverse).astype(jnp.bfloat16)
                mixed[at.z, pl.ds(first, half), cols] = jnp.dot(
                    weights, values, preferred_element_type=jnp.float32).astype(jnp.bfloat16)

    def relay_inner(h):
        @pl.when(at.z == 1)
        def _():
            line_m.falling(1, h)

        @pl.when(at.z == 2)
        def _():
            line_m.rising(1, h)

    def relay_outer(s, h):
        @pl.when(at.z == (1 if s == 1 else 2))
        def _():
            line_m.rising(s, h)

        @pl.when(at.z == (2 if s == 1 else 1))
        def _():
            line_m.falling(s, h)

    project_q(0)
    project_q(1)

    @pl.when(outer)
    def _():
        plane_o[0].first()

    for h in range(heads):
        if h > 1:
            cols = slice(h * 256, (h + 1) * 256)
            total[:, cols] = jnp.zeros((rows, 256), jnp.float32)
            project_part(h, lambda chip: chip != at.chip_d)

            @pl.when(inner)
            def _():
                plane_q[h].third()

            project_part(h, lambda chip: chip == at.chip_d)
            for g in range(2 * h, 2 * h + 2):
                cols = slice(g * 128, (g + 1) * 128)
                mixed[at.z, :, cols] = head(total[:, cols], gain_q[...])
        if h > 1:
            @pl.when(inner)
            def _():
                relay_inner(h - 1)

        halo.need(h)
        attend_head(h)
        line_m.start(h)

        @pl.when(inner)
        def _():
            if h == 1:
                plane_q[2].first()
                plane_q[3].start()
                relay_inner(0)
                plane_q[2].second()
                plane_q[2].sister()
            if h == 2:
                plane_q[3].first()
                plane_o[0].start()
                plane_o[1].start()
                plane_q[3].second()
                plane_q[3].sister()
            if h == 3:
                plane_o[0].first()
                relay_inner(3)

    def output(tile, p):
        some = pl.ds(tile * wide, wide)

        def step(j, _):
            total_o[some, :] += lax.dot_general(
                o_all[j * 2 + p, some, :], mixed[j, :, p * (nq // 2):(p + 1) * (nq // 2)],
                (((1,), (1,)), ((), ())), preferred_element_type=jnp.float32)
        return step

    last = jnp.where(at.z < 2, 3, 0)

    @pl.when(inner)
    def _():
        relay_outer(1, 0)
        relay_outer(1, 1)
        relay_outer(2, 0)
        plane_o[0].second()
        relay_outer(1, 2)
        relay_outer(2, 1)
        relay_outer(1, 3)
        relay_outer(2, 2)
        plane_o[1].first()
        relay_outer(2, 3)

    @pl.when(outer)
    def _():
        plane_o[0].second()
        for s in (1, 2):
            for h in range(heads):
                line_m.step(s, h)
        plane_o[1].first()

    plane_o[0].sister()

    def store(tile):
        some = pl.ds(tile * wide, wide)
        result[some, :] = total_o[some, :].astype(jnp.bfloat16)
        one = pltpu.make_async_copy(result.at[some], out.at[some], local.at[8 + tile])
        one.start()
        return one

    early = lambda j: (j != at.chip_d) & (inner | (j != last))
    far = lambda j: outer & (j == last) & (j != at.chip_d)
    each(early, (0,), output(0, 0), output(0, 1))
    plane_o[1].second()
    plane_o[1].sister()
    each(early, (0,), output(1, 0), output(1, 1))
    line_m.step(3, 0)
    line_m.step(3, 1)
    each(far, (0,), output(0, 0), output(1, 0))
    plane_o[0].third()
    each(lambda j: (j == at.chip_d) & (inner | (j != last)), (0,), output(0, 0), output(0, 1))
    line_m.step(3, 2)
    line_m.step(3, 3)
    each(far, (0,), output(0, 1), output(1, 1))
    each(lambda j: outer & (j == last) & (j == at.chip_d), (0,), output(0, 0), output(0, 1))
    stores = [store(0)]
    plane_o[1].third()
    each(lambda j: j == at.chip_d, (0,), output(1, 0), output(1, 1))
    stores.append(store(1))
    line.finish()
    line_m.finish()
    for plane in [plane_k] + plane_q + plane_o:
        plane.finish()
    halo.finish()
    for one in stores:
        one.wait()


def fused(tokens, w_query, key_weight, value_weight, w_output, query_gain, key_gain):
    rows, depth = tokens.shape
    nq, nk = w_query.shape[1], key_weight.shape[1]
    features = w_output.shape[1]
    freqs = 10000.0 ** (-(jnp.arange(64, dtype=jnp.float32) * 2.0 / HEAD_SIZE))
    freqs = freqs.reshape(1, HEAD_SIZE // 2)
    hbm = pl.BlockSpec(memory_space=pl.ANY)
    bf16, dma = jnp.bfloat16, pltpu.SemaphoreType.DMA
    return pl.pallas_call(
        kernel,
        out_shape=jax.ShapeDtypeStruct((features, rows), bf16),
        in_specs=[hbm] * 8,
        out_specs=hbm,
        scratch_shapes=[
            pltpu.VMEM((4, depth, rows), bf16),
            pltpu.VMEM((8, rows, depth // 2), bf16),
            pltpu.VMEM((4 * depth, 2 * nk), bf16),
            pltpu.VMEM((nq // 256, 4 * depth, 256), bf16),
            pltpu.VMEM((rows, 2 * nk), jnp.float32),
            pltpu.VMEM((8, features, nq // 2), bf16),
            pltpu.VMEM((4, rows, nq), bf16),
            pltpu.VMEM((3 * rows, 2 * nk), bf16),
            pltpu.VMEM((features, rows), jnp.float32),
            pltpu.VMEM((2, rows // 2, rows // 2 + WINDOW_KEYS), jnp.float32),
            pltpu.VMEM((features, rows), bf16),
            pltpu.VMEM((rows, HEAD_SIZE), jnp.float32),
            pltpu.VMEM((rows, HEAD_SIZE), jnp.float32),
            pltpu.VMEM((1, HEAD_SIZE), jnp.float32),
            pltpu.VMEM((1, HEAD_SIZE), jnp.float32),
            pltpu.VMEM((1, HEAD_SIZE // 2), jnp.float32),
            dma((2,)), dma((4, 2)), dma((1,)), dma((7,)), dma((4, 1)), dma((4, 7)),
            dma((2,)), dma((4, 4)), dma((2, 1)), dma((2, 7)), dma((2,)), dma((2, 4)), dma((10,)),
        ],
        compiler_params=pltpu.CompilerParams(
            collective_id=0, has_side_effects=True, vmem_limit_bytes=62 * MIB),
    )(tokens.T, w_query, key_weight, value_weight, w_output.T,
      query_gain.reshape(1, HEAD_SIZE), key_gain.reshape(1, HEAD_SIZE), freqs).T


def solution(mesh):
    small = dict(mesh.shape) == {"seq": 2, "row": 4, "col": 4}
    split = P(("seq", "row"), "col")
    return jax.shard_map(
        fused if small else shards,
        mesh=mesh,
        in_specs=(split, split, split, split, split, P(), P()),
        out_specs=split,
        check_vma=False,
    )
```
